32 devices in a mesh: wide: 8 (over z, x), narrow: 4 (over y, core).
Axes of the slice: x: 2, y: 2, z: 4, core: 2. Of those that a mesh axis runs over, the one named last changes fastest.
Arguments:
- tokens: bfloat16 [2, 2048, 2048], P(None, ('wide', 'narrow')), may hold values from -6 to 6
- lengths: int32 [2, 32], P(None, ('wide', 'narrow')), may hold values from 48 to 64, as said below
- cotangent: bfloat16 [2, 2048, 2048], P(None, ('wide', 'narrow')), may hold values from -6 to 6
- norm1_gain: bfloat16 [2048], P(('wide', 'narrow')), may hold values from 0.5 to 1.5
- query_weight: bfloat16 [2048, 2048], P(('wide', 'narrow')), may hold values from -0.125 to 0.125
- key_weight: bfloat16 [2048, 2048], P(('wide', 'narrow')), may hold values from -0.125 to 0.125
- value_weight: bfloat16 [2048, 2048], P(('wide', 'narrow')), may hold values from -0.125 to 0.125
- out_weight: bfloat16 [2048, 2048], P(('wide', 'narrow')), may hold values from -0.375 to 0.375
- norm2_gain: bfloat16 [2048], P(('wide', 'narrow')), may hold values from 0.5 to 1.5
- gate_weight: bfloat16 [2048, 8192], P(('wide', 'narrow')), may hold values from -0.125 to 0.125
- up_weight: bfloat16 [2048, 8192], P(('wide', 'narrow')), may hold values from -0.125 to 0.125
- down_weight: bfloat16 [8192, 2048], P(('wide', 'narrow')), may hold values from -0.0625 to 0.0625
Outputs:
- layer_output: bfloat16 [2, 2048, 2048], P(None, ('wide', 'narrow'))
- input_grad: float32 [2, 2048, 2048], P(None, ('wide', 'narrow'))
- norm1_gain_grad: float32 [2048], P(('wide', 'narrow'))
- query_grad: float32 [2048, 2048], P(('wide', 'narrow'))
- key_grad: float32 [2048, 2048], P(('wide', 'narrow'))
- value_grad: float32 [2048, 2048], P(('wide', 'narrow'))
- out_grad: float32 [2048, 2048], P(('wide', 'narrow'))
- norm2_gain_grad: float32 [2048], P(('wide', 'narrow'))
- gate_grad: float32 [2048, 8192], P(('wide', 'narrow'))
- up_grad: float32 [2048, 8192], P(('wide', 'narrow'))
- down_grad: float32 [8192, 2048], P(('wide', 'narrow'))
The draws below stay inside these ranges and needn't reach their ends.
Inputs may be any that keep to these rules, and one draw needn't show every extreme that they name: `lengths`: in every micro-batch one sequence has all 64 tokens valid and another has 48.
All inputs are finite; a program needn't handle non-finite values.
Results may differ from the reference program's by a relative error of at most 0.014.
Values may be sent and summed in bfloat16 or wider, within the bound.
A program may use at most 512 MiB of HBM per device.

```python
import math
import jax
import jax.numpy as jnp
from jax import lax

D = 2048
HEAD_DIM = 128
FF = 8192
SEQ = 64
MB = 2
SEQS = 32
ROWS = 2048


def draw_lengths(key, part):
    shortest = SEQ - SEQ // 4
    counts = jax.random.randint(jax.random.fold_in(key, 101), (MB, SEQS), shortest, SEQ + 1)
    full_slot = jax.random.randint(jax.random.fold_in(key, 202), (MB, 1), 0, SEQS)
    offset = jax.random.randint(jax.random.fold_in(key, 303), (MB, 1), 1, SEQS)
    short_slot = (full_slot + offset) % SEQS
    column = jnp.arange(SEQS)[None, :]
    counts = jnp.where(column == full_slot, SEQ, counts)
    counts = jnp.where(column == short_slot, shortest, counts)
    return counts.astype(jnp.int32)


def block_scale(own_key, shape, split, low, largest):
    def one(dim, blocks):
        heights = jax.random.uniform(jax.random.fold_in(jax.random.fold_in(own_key, 6), dim), (blocks,), jnp.float32, low / len(split), largest / len(split))
        return jnp.repeat(jnp.exp(heights), shape[dim] // blocks).reshape((-1,) + (1,) * (len(shape) - dim - 1))

    factor_of = one(*split[0])
    for cut in split[1:]:
        factor_of = factor_of * one(*cut)
    return factor_of


def normal_values(stream_key, extent, deviation, bound, pieces=(), held_as=jnp.bfloat16):
    entries = deviation * jax.random.normal(stream_key, extent, jnp.float32)
    if pieces:
        entries = entries * block_scale(stream_key, extent, pieces, -0.22, 0.18)
    return jnp.clip(entries, -bound, bound).astype(held_as)


def setup_inputs(seed: int = 0) -> dict:
    seeds = jax.random.split(jax.random.key(seed), 13)
    return {
        "tokens": normal_values(seeds[0], (MB, ROWS, D), 1.0, 6.0, ((1, 32),)),
        "lengths": draw_lengths(jax.random.fold_in(seeds[12], 71), 0),
        "cotangent": normal_values(seeds[2], (MB, ROWS, D), 1.0, 6.0, ((1, 32),)),
        "norm1_gain": jnp.clip(1.0 + 0.1 * jax.random.normal(seeds[3], (D,), jnp.float32), 0.5, 1.5).astype(jnp.bfloat16),
        "query_weight": normal_values(seeds[4], (D, D), D ** -0.5, 0.125, ((0, 32),)),
        "key_weight": normal_values(seeds[5], (D, D), D ** -0.5, 0.125, ((0, 32),)),
        "value_weight": normal_values(seeds[6], (D, D), D ** -0.5, 0.125, ((0, 32),)),
        "out_weight": normal_values(seeds[7], (D, D), (D * 8 // SEQ) ** -0.5, 0.375, ((0, 32),)),
        "norm2_gain": jnp.clip(1.0 + 0.1 * jax.random.normal(seeds[8], (D,), jnp.float32), 0.5, 1.5).astype(jnp.bfloat16),
        "gate_weight": normal_values(seeds[9], (D, FF), D ** -0.5, 0.125, ((0, 32),)),
        "up_weight": normal_values(seeds[10], (D, FF), D ** -0.5, 0.125, ((0, 32),)),
        "down_weight": normal_values(seeds[11], (FF, D), FF ** -0.5, 0.0625, ((0, 32),)),
    }


epsilon = 1e-05
rope_base = 10000.0
highest = lax.Precision.HIGHEST

@jax.custom_vjp
def low(v):
    return lax.optimization_barrier(v.astype(jnp.bfloat16)).astype(jnp.float32)

@jax.custom_vjp
def low_back(v):
    return v

def low_keep(v):
    return (low(v), None)

def low_pass(kept, grad):
    return (grad,)

def back_keep(v):
    return (v, None)

def back_low(kept, grad):
    return (low(grad),)
low.defvjp(low_keep, low_pass)
low_back.defvjp(back_keep, back_low)

def precise_dot(left, right):
    return jnp.dot(left, right, precision=highest, preferred_element_type=jnp.float32)

def rotation_tables(length):
    half_size = HEAD_DIM // 2
    position = jnp.arange(length).astype(jnp.float32)
    frequency = rope_base ** (-jnp.arange(half_size).astype(jnp.float32) / half_size)
    angles = position[:, None] * frequency[None, :]
    return (jnp.cos(angles), jnp.sin(angles))

def rotate(values, cosine, sine_table):
    half_size = values.shape[-1] // 2
    front_half = values[..., :half_size]
    back_half = values[..., half_size:]
    cos_wide = cosine[:, None, :]
    sin_wide = sine_table[:, None, :]
    return jnp.concatenate([front_half * cos_wide - back_half * sin_wide, back_half * cos_wide + front_half * sin_wide], axis=-1)

def rms_norm(values, gain_vector):
    inverse = lax.rsqrt(lax.optimization_barrier(jnp.mean(values * values, axis=-1, keepdims=True)) + epsilon)
    return values * inverse * gain_vector

def layer(inputs, params, row_mask):
    norm1_gain, query_weight, key_weight, value_weight, out_weight, norm2_gain, gate_weight, up_weight, down_weight = params
    groups, length, model_width = inputs.shape
    heads_count = model_width // HEAD_DIM
    cosine, sine_table = rotation_tables(length)
    normed = low(rms_norm(inputs, norm1_gain)).reshape(groups * length, model_width)

    def project(weight):
        return precise_dot(normed, weight).reshape(groups, length, heads_count, HEAD_DIM)
    queries = low(rotate(low_back(project(query_weight)), cosine, sine_table))
    keys_rot = low(rotate(low_back(project(key_weight)), cosine, sine_table))
    values_all = low(low_back(project(value_weight)))
    scores = jnp.einsum('gqhd,gkhd->ghqk', queries, keys_rot, precision=highest) * HEAD_DIM ** (-0.5) - math.log(length)
    causal = (jnp.arange(length)[:, None] >= jnp.arange(length)[None, :]).astype(jnp.float32)
    sigmoid_weights = low(jax.nn.sigmoid(low_back(scores)) * causal)
    attended = jnp.einsum('ghqk,gkhd->gqhd', sigmoid_weights, values_all, precision=highest)
    attended = low(low_back(attended)).reshape(groups * length, model_width)
    branch = low_back(precise_dot(attended, out_weight)).reshape(groups, length, model_width)
    middle = inputs + branch
    normed_two = low(rms_norm(middle, norm2_gain)).reshape(groups * length, model_width)
    gate_value = low_back(precise_dot(normed_two, gate_weight))
    up_value = low_back(precise_dot(normed_two, up_weight))
    hidden = low(jax.nn.silu(gate_value) * up_value)
    feed_out = low_back(precise_dot(hidden, down_weight)).reshape(groups, length, model_width)
    return (middle + feed_out) * row_mask[:, :, None]

def reference(tokens, lengths, cotangent, norm1_gain, query_weight, key_weight, value_weight, out_weight, norm2_gain, gate_weight, up_weight, down_weight):
    sequences = MB * SEQS
    group_size = min(sequences, max(1, 4096 // SEQ))
    rounds = sequences // group_size
    inputs = tokens.astype(jnp.float32).reshape(rounds, group_size, SEQ, D)
    cotangents = cotangent.astype(jnp.float32).reshape(rounds, group_size, SEQ, D)
    valid_counts = lengths.astype(jnp.int32).reshape(rounds, group_size)
    params = tuple((weight.astype(jnp.float32) for weight in (norm1_gain, query_weight, key_weight, value_weight, out_weight, norm2_gain, gate_weight, up_weight, down_weight)))
    position = jnp.arange(SEQ, dtype=jnp.int32)

    def one_round(running, round_item):
        block_inputs, block_cot, block_lengths = round_item
        row_mask = (position[None, :] < block_lengths[:, None]).astype(jnp.float32)
        result, pullback = jax.vjp(lambda values, weights: layer(values, weights, row_mask), block_inputs, params)
        input_part, weight_parts = pullback(block_cot)
        running = tuple((summed + grad_part for summed, grad_part in zip(running, weight_parts)))
        return (running, (result.astype(jnp.bfloat16), input_part))
    initial = tuple((jnp.zeros(weight.shape, jnp.float32) for weight in params))
    running, (results, input_parts) = lax.scan(one_round, initial, (inputs, cotangents, valid_counts))
    layer_output = results.reshape(MB, ROWS, D)
    input_grad = input_parts.reshape(MB, ROWS, D)
    return (layer_output, input_grad, running[0], running[1], running[2], running[3], running[4], running[5], running[6], running[7], running[8])
```

```python
import functools
import math

import jax
import jax.numpy as jnp
from jax import lax
from jax.sharding import PartitionSpec as P

HEAD_DIM = 128


epsilon = 1e-05
rope_base = 10000.0


def mixed_dot(left, right):
    return jnp.dot(left, right, preferred_element_type=jnp.float32)


def outer_dot(left, right):
    return lax.dot_general(
        left, right, (((0,), (0,)), ((), ())), preferred_element_type=jnp.float32
    )


def back_dot(left, right):
    return lax.dot_general(
        left, right, (((1,), (1,)), ((), ())), preferred_element_type=jnp.float32
    )


def joined(pieces):
    return jnp.concatenate(pieces, axis=0)


def rotation_tables(length):
    half_size = HEAD_DIM // 2
    position = jnp.arange(length).astype(jnp.float32)
    frequency = rope_base ** (-jnp.arange(half_size).astype(jnp.float32) / half_size)
    angles = position[:, None] * frequency[None, :]
    return (jnp.cos(angles), jnp.sin(angles))


def rotate(values, cosine, sine_table):
    half_size = values.shape[-1] // 2
    front_half = values[..., :half_size]
    back_half = values[..., half_size:]
    cos_wide = cosine[:, None, :]
    sin_wide = sine_table[:, None, :]
    return jnp.concatenate(
        [
            front_half * cos_wide - back_half * sin_wide,
            back_half * cos_wide + front_half * sin_wide,
        ],
        axis=-1,
    )


def norm_back(grad_normed, normed, inverse):
    return inverse * (grad_normed - normed * jnp.mean(grad_normed * normed, axis=-1, keepdims=True))


def score_gates(queries, keys_rot):
    length = queries.shape[0]
    scores = jnp.einsum(
        "qhd,khd->hqk", queries, keys_rot, preferred_element_type=jnp.float32
    ) * HEAD_DIM ** (-0.5) - math.log(length)
    causal = (jnp.arange(length)[:, None] >= jnp.arange(length)[None, :]).astype(jnp.float32)
    return (jax.nn.sigmoid(scores), causal)


def attention_forward(inputs, attend_full):
    norm_gain, query_weight, key_weight, value_weight, out_weight = attend_full
    length, model_width = inputs.shape
    heads_count = model_width // HEAD_DIM
    floats = inputs.astype(jnp.float32)
    inverse = lax.rsqrt(jnp.mean(floats * floats, axis=-1, keepdims=True) + epsilon)
    normed = floats * inverse
    lowered = (normed * norm_gain.astype(jnp.float32)).astype(jnp.bfloat16)
    cosine, sine_table = rotation_tables(length)
    queries = rotate(
        mixed_dot(lowered, query_weight).reshape(length, heads_count, HEAD_DIM), cosine, sine_table
    ).astype(jnp.bfloat16)
    keys_rot = rotate(
        mixed_dot(lowered, key_weight).reshape(length, heads_count, HEAD_DIM), cosine, sine_table
    ).astype(jnp.bfloat16)
    values_all = (
        mixed_dot(lowered, value_weight).astype(jnp.bfloat16).reshape(length, heads_count, HEAD_DIM)
    )
    gates_sig, causal = score_gates(queries, keys_rot)
    weights_low = (gates_sig * causal).astype(jnp.bfloat16)
    attended = jnp.einsum(
        "hqk,khd->qhd", weights_low, values_all, preferred_element_type=jnp.float32
    )
    attended = attended.astype(jnp.bfloat16).reshape(length, model_width)
    middle = floats + mixed_dot(attended, out_weight)
    return (middle, (inverse, normed, lowered, queries, keys_rot, values_all, attended))


def feed_front(middle, front_full):
    norm_gain, gate_weight, up_weight = front_full
    inverse = lax.rsqrt(jnp.mean(middle * middle, axis=-1, keepdims=True) + epsilon)
    normed = middle * inverse
    lowered = (normed * norm_gain.astype(jnp.float32)).astype(jnp.bfloat16)
    gate_value = mixed_dot(lowered, gate_weight)
    up_value = mixed_dot(lowered, up_weight)
    hidden = (jax.nn.silu(gate_value) * up_value).astype(jnp.bfloat16)
    return (hidden, (inverse, normed, lowered, gate_value, up_value, hidden))


def attention_backward(grad_middle, saved_state, attend_full):
    norm_gain, query_weight, key_weight, value_weight, out_weight = attend_full
    inverse, normed, lowered, queries, keys_rot, values_all, attended = saved_state
    length, model_width = grad_middle.shape
    heads_count = model_width // HEAD_DIM
    grad_low = grad_middle.astype(jnp.bfloat16)
    grad_attended = (
        back_dot(grad_low, out_weight).astype(jnp.bfloat16).reshape(length, heads_count, HEAD_DIM)
    )
    gates_sig, causal = score_gates(queries, keys_rot)
    weights_low = (gates_sig * causal).astype(jnp.bfloat16)
    grad_weights = jnp.einsum(
        "qhd,khd->hqk", grad_attended, values_all, preferred_element_type=jnp.float32
    )
    grad_values = jnp.einsum(
        "hqk,qhd->khd", weights_low, grad_attended, preferred_element_type=jnp.float32
    )
    grad_values = grad_values.astype(jnp.bfloat16).reshape(length, model_width)
    grad_scores = (grad_weights * gates_sig * (1.0 - gates_sig) * causal).astype(jnp.bfloat16)
    scale_factor = HEAD_DIM ** (-0.5)
    cosine, sine_table = rotation_tables(length)
    query_rot = (
        jnp.einsum("hqk,khd->qhd", grad_scores, keys_rot, preferred_element_type=jnp.float32)
        * scale_factor
    )
    key_rot = (
        jnp.einsum("hqk,qhd->khd", grad_scores, queries, preferred_element_type=jnp.float32)
        * scale_factor
    )
    grad_queries = (
        rotate(query_rot, cosine, -sine_table).astype(jnp.bfloat16).reshape(length, model_width)
    )
    grad_keys = (
        rotate(key_rot, cosine, -sine_table).astype(jnp.bfloat16).reshape(length, model_width)
    )
    grad_lowered = (
        back_dot(grad_queries, query_weight)
        + back_dot(grad_keys, key_weight)
        + back_dot(grad_values, value_weight)
    )
    gain_term = jnp.sum(grad_lowered * normed, axis=0)
    grad_inputs = grad_middle + norm_back(
        grad_lowered * norm_gain.astype(jnp.float32), normed, inverse
    )
    return (grad_inputs, gain_term, (grad_queries, grad_keys, grad_values, grad_low))


def gathered_plan(
    tokens,
    lengths,
    cotangent,
    norm1_gain,
    query_weight,
    key_weight,
    value_weight,
    out_weight,
    norm2_gain,
    gate_weight,
    up_weight,
    down_weight,
):
    micro_count = tokens.shape[0]
    length = tokens.shape[1]
    position = jnp.arange(length, dtype=jnp.int32)
    row_masks = [
        (position < lengths[micro_index, 0]).astype(jnp.float32)
        for micro_index in range(micro_count)
    ]
    attend_full = (
        lax.all_gather(norm1_gain, ("wide", "narrow"), axis=0, tiled=True),
        lax.all_gather(query_weight, ("wide", "narrow"), axis=0, tiled=True),
        lax.all_gather(key_weight, ("wide", "narrow"), axis=0, tiled=True),
        lax.all_gather(value_weight, ("wide", "narrow"), axis=0, tiled=True),
        lax.all_gather(out_weight, ("wide", "narrow"), axis=0, tiled=True),
    )
    middles = []
    attend_states = []
    for micro_index in range(micro_count):
        middle, attend_state = attention_forward(tokens[micro_index], attend_full)
        middles.append(middle)
        attend_states.append(attend_state)
    front_full = (
        lax.all_gather(norm2_gain, ("wide", "narrow"), axis=0, tiled=True),
        lax.all_gather(gate_weight, ("wide", "narrow"), axis=0, tiled=True),
        lax.all_gather(up_weight, ("wide", "narrow"), axis=0, tiled=True),
    )
    feed_states = []
    for micro_index in range(micro_count):
        hidden, feed_state = feed_front(middles[micro_index], front_full)
        feed_states.append(feed_state)
    down_full = lax.all_gather(down_weight, ("wide", "narrow"), axis=0, tiled=True)
    layer_rows = []
    for micro_index in range(micro_count):
        result = (
            middles[micro_index] + mixed_dot(feed_states[micro_index][5], down_full)
        ) * row_masks[micro_index][:, None]
        layer_rows.append(result.astype(jnp.bfloat16))
    down_back = lax.all_gather(down_weight, ("wide", "narrow"), axis=0, tiled=True)
    upstreams = []
    upstream_lows = []
    grad_gates = []
    grad_ups = []
    for micro_index in range(micro_count):
        inverse, normed, lowered, gate_value, up_value, hidden = feed_states[micro_index]
        upstream = cotangent[micro_index].astype(jnp.float32) * row_masks[micro_index][:, None]
        upstream_low = upstream.astype(jnp.bfloat16)
        grad_hidden = back_dot(upstream_low, down_back)
        gate_sig = jax.nn.sigmoid(gate_value)
        grad_gates.append(
            (grad_hidden * up_value * gate_sig * (1.0 + gate_value * (1.0 - gate_sig))).astype(
                jnp.bfloat16
            )
        )
        grad_ups.append((grad_hidden * gate_value * gate_sig).astype(jnp.bfloat16))
        upstreams.append(upstream)
        upstream_lows.append(upstream_low)
    hidden_rows = joined([state[5] for state in feed_states])
    lowered_rows = joined([state[2] for state in feed_states])
    down_sum = lax.psum_scatter(
        outer_dot(hidden_rows, joined(upstream_lows)),
        ("wide", "narrow"),
        scatter_dimension=0,
        tiled=True,
    )
    gain_two, gate_back = (
        lax.all_gather(norm2_gain, ("wide", "narrow"), axis=0, tiled=True),
        lax.all_gather(gate_weight, ("wide", "narrow"), axis=0, tiled=True),
    )
    grad_loweds = [
        back_dot(grad_gates[micro_index], gate_back) for micro_index in range(micro_count)
    ]
    gate_sum = lax.psum_scatter(
        outer_dot(lowered_rows, joined(grad_gates)),
        ("wide", "narrow"),
        scatter_dimension=0,
        tiled=True,
    )
    up_back = lax.all_gather(up_weight, ("wide", "narrow"), axis=0, tiled=True)
    gain_total = jnp.zeros((tokens.shape[2],), jnp.float32)
    grad_middles = []
    for micro_index in range(micro_count):
        inverse, normed, lowered, gate_value, up_value, hidden = feed_states[micro_index]
        grad_lowered = grad_loweds[micro_index] + back_dot(grad_ups[micro_index], up_back)
        gain_total = gain_total + jnp.sum(grad_lowered * normed, axis=0)
        grad_middles.append(
            upstreams[micro_index]
            + norm_back(grad_lowered * gain_two.astype(jnp.float32), normed, inverse)
        )
    up_total = outer_dot(lowered_rows, joined(grad_ups))
    gain_two_sum, up_sum = (
        lax.psum_scatter(gain_total, ("wide", "narrow"), scatter_dimension=0, tiled=True),
        lax.psum_scatter(up_total, ("wide", "narrow"), scatter_dimension=0, tiled=True),
    )
    attend_back = (
        lax.all_gather(norm1_gain, ("wide", "narrow"), axis=0, tiled=True),
        lax.all_gather(query_weight, ("wide", "narrow"), axis=0, tiled=True),
        lax.all_gather(key_weight, ("wide", "narrow"), axis=0, tiled=True),
        lax.all_gather(value_weight, ("wide", "narrow"), axis=0, tiled=True),
        lax.all_gather(out_weight, ("wide", "narrow"), axis=0, tiled=True),
    )
    input_rows = []
    gain_first = jnp.zeros((tokens.shape[2],), jnp.float32)
    grad_lists = ([], [], [], [])
    for micro_index in range(micro_count):
        grad_inputs, gain_term, row_grads = attention_backward(
            grad_middles[micro_index], attend_states[micro_index], attend_back
        )
        input_rows.append(grad_inputs)
        gain_first = gain_first + gain_term
        for slot_index in range(4):
            grad_lists[slot_index].append(row_grads[slot_index])
    first_rows = joined([state[2] for state in attend_states])
    attended_rows = joined([state[6] for state in attend_states])
    query_total = outer_dot(first_rows, joined(grad_lists[0]))
    key_total = outer_dot(first_rows, joined(grad_lists[1]))
    value_total = outer_dot(first_rows, joined(grad_lists[2]))
    out_total = outer_dot(attended_rows, joined(grad_lists[3]))
    attend_sums = (
        lax.psum_scatter(gain_first, ("wide", "narrow"), scatter_dimension=0, tiled=True),
        lax.psum_scatter(query_total, ("wide", "narrow"), scatter_dimension=0, tiled=True),
        lax.psum_scatter(key_total, ("wide", "narrow"), scatter_dimension=0, tiled=True),
        lax.psum_scatter(value_total, ("wide", "narrow"), scatter_dimension=0, tiled=True),
        lax.psum_scatter(out_total, ("wide", "narrow"), scatter_dimension=0, tiled=True),
    )
    layer_output = jnp.stack(layer_rows)
    input_grad = jnp.stack(input_rows)
    return (
        layer_output,
        input_grad,
        attend_sums[0],
        attend_sums[1],
        attend_sums[2],
        attend_sums[3],
        attend_sums[4],
        gain_two_sum,
        gate_sum,
        up_sum,
        down_sum,
    )


def gather_rows(block):
    return lax.all_gather(block, "wide", axis=0, tiled=True)


def scatter_rows(partial):
    return lax.psum_scatter(
        partial.astype(jnp.bfloat16), "wide", scatter_dimension=0, tiled=True
    ).astype(jnp.float32)


def to_columns(weights, wide):
    pieces = [w.reshape(w.shape[0], wide, w.shape[1] // wide) for w in weights]
    block = jnp.swapaxes(jnp.concatenate(pieces, axis=2), 0, 1)
    block = lax.all_to_all(block, "wide", split_axis=0, concat_axis=0, tiled=True)
    full = lax.all_gather(block, "narrow", axis=1, tiled=True)
    return full.reshape(-1, full.shape[2])


def to_rows(columns, wide, narrow):
    rows, width = columns.shape
    block = columns.astype(jnp.bfloat16).reshape(wide, rows // wide, width)
    block = lax.psum_scatter(block, "narrow", scatter_dimension=1, tiled=True)
    return lax.all_to_all(block, "wide", split_axis=0, concat_axis=0, tiled=True)


def own_rows(block, start, width):
    piece = block[:, :, start : start + width]
    return jnp.swapaxes(piece, 0, 1).reshape(piece.shape[1], -1).astype(jnp.float32)


def gather_narrow(weight):
    return lax.all_gather(weight, "narrow", axis=0, tiled=True)


def sum_narrow(partial):
    return lax.psum_scatter(
        partial.astype(jnp.bfloat16), "narrow", scatter_dimension=0, tiled=True
    ).astype(jnp.float32)


def rotate_heads(values, cosine, sine_table):
    half_size = HEAD_DIM // 2
    front_half = values[..., :half_size]
    back_half = values[..., half_size:]
    return jnp.concatenate(
        [
            front_half * cosine - back_half * sine_table,
            back_half * cosine + front_half * sine_table,
        ],
        axis=-1,
    )


def split_plan(
    wide,
    narrow,
    tokens,
    lengths,
    cotangent,
    norm1_gain,
    query_weight,
    key_weight,
    value_weight,
    out_weight,
    norm2_gain,
    gate_weight,
    up_weight,
    down_weight,
):
    micro_count, length, width = tokens.shape
    rows = micro_count * length
    sequences = wide * micro_count
    heads = width // HEAD_DIM // wide
    head_width = heads * HEAD_DIM
    hidden_width = gate_weight.shape[1] // wide
    position = jnp.arange(length, dtype=jnp.int32)
    row_mask = (position[None, :] < lengths).astype(jnp.float32).reshape(rows, 1)

    gains = lax.all_gather(
        jnp.stack([norm1_gain, norm2_gain]), ("wide", "narrow"), axis=1, tiled=True
    ).astype(jnp.float32)
    attend_columns = to_columns((query_weight, key_weight, value_weight), wide)

    floats = tokens.reshape(rows, width).astype(jnp.float32)
    inverse_one = lax.rsqrt(jnp.mean(floats * floats, axis=-1, keepdims=True) + epsilon)
    normed_one = floats * inverse_one
    first_all = gather_rows((normed_one * gains[0]).astype(jnp.bfloat16))
    feed_columns = to_columns((gate_weight, up_weight), wide)
    out_rows = gather_narrow(out_weight)
    down_rows = gather_narrow(down_weight)

    cosine, sine_table = rotation_tables(length)
    cosine, sine_table = cosine[None, :, None, :], sine_table[None, :, None, :]
    joint = mixed_dot(first_all, attend_columns)
    by_head = (sequences, length, heads, HEAD_DIM)
    queries = rotate_heads(joint[:, :head_width].reshape(by_head), cosine, sine_table).astype(
        jnp.bfloat16
    )
    keys_rot = rotate_heads(
        joint[:, head_width : 2 * head_width].reshape(by_head), cosine, sine_table
    ).astype(jnp.bfloat16)
    values_all = joint[:, 2 * head_width :].reshape(by_head).astype(jnp.bfloat16)
    scores = jnp.einsum(
        "sqhd,skhd->shqk", queries, keys_rot, preferred_element_type=jnp.float32
    ) * HEAD_DIM ** (-0.5) - math.log(length)
    causal = (position[:, None] >= position[None, :]).astype(jnp.float32)
    gates_sig = jax.nn.sigmoid(scores)
    weights_low = (gates_sig * causal).astype(jnp.bfloat16)
    attended = (
        jnp.einsum("shqk,skhd->sqhd", weights_low, values_all, preferred_element_type=jnp.float32)
        .astype(jnp.bfloat16)
        .reshape(sequences * length, head_width)
    )
    middle = floats + scatter_rows(mixed_dot(attended, out_rows))

    inverse_two = lax.rsqrt(jnp.mean(middle * middle, axis=-1, keepdims=True) + epsilon)
    normed_two = middle * inverse_two
    second_all = gather_rows((normed_two * gains[1]).astype(jnp.bfloat16))
    upstream = cotangent.reshape(rows, width).astype(jnp.float32) * row_mask
    upstream_all = gather_rows(upstream.astype(jnp.bfloat16))

    front = mixed_dot(second_all, feed_columns)
    gate_value = front[:, :hidden_width]
    up_value = front[:, hidden_width:]
    gate_sig = jax.nn.sigmoid(gate_value)
    hidden = (gate_value * gate_sig * up_value).astype(jnp.bfloat16)
    feed_out = scatter_rows(mixed_dot(hidden, down_rows))
    layer_output = ((middle + feed_out) * row_mask).astype(jnp.bfloat16)

    grad_hidden = back_dot(upstream_all, down_rows)
    grad_gate = (
        grad_hidden * up_value * gate_sig * (1.0 + gate_value * (1.0 - gate_sig))
    ).astype(jnp.bfloat16)
    grad_up = (grad_hidden * gate_value * gate_sig).astype(jnp.bfloat16)
    grad_front = jnp.concatenate([grad_gate, grad_up], axis=1)
    grad_second = scatter_rows(back_dot(grad_front, feed_columns))
    down_grad = sum_narrow(outer_dot(hidden, upstream_all))
    front_block = to_rows(outer_dot(second_all, grad_front), wide, narrow)
    gate_grad = own_rows(front_block, 0, hidden_width)
    up_grad = own_rows(front_block, hidden_width, hidden_width)

    gain_two = jnp.sum(grad_second * normed_two, axis=0)
    grad_middle = upstream + norm_back(grad_second * gains[1], normed_two, inverse_two)
    middle_all = gather_rows(grad_middle.astype(jnp.bfloat16))

    grad_attended = back_dot(middle_all, out_rows).astype(jnp.bfloat16).reshape(by_head)
    out_grad = sum_narrow(outer_dot(attended, middle_all))
    grad_weights = jnp.einsum(
        "sqhd,skhd->shqk", grad_attended, values_all, preferred_element_type=jnp.float32
    )
    grad_values = jnp.einsum(
        "shqk,sqhd->skhd", weights_low, grad_attended, preferred_element_type=jnp.float32
    ).astype(jnp.bfloat16)
    grad_scores = (grad_weights * gates_sig * (1.0 - gates_sig) * causal).astype(jnp.bfloat16)
    scale_factor = HEAD_DIM ** (-0.5)
    query_rot = (
        jnp.einsum("shqk,skhd->sqhd", grad_scores, keys_rot, preferred_element_type=jnp.float32)
        * scale_factor
    )
    key_rot = (
        jnp.einsum("shqk,sqhd->skhd", grad_scores, queries, preferred_element_type=jnp.float32)
        * scale_factor
    )
    flat = (sequences * length, head_width)
    grad_joint = jnp.concatenate(
        [
            rotate_heads(query_rot, cosine, -sine_table).astype(jnp.bfloat16).reshape(flat),
            rotate_heads(key_rot, cosine, -sine_table).astype(jnp.bfloat16).reshape(flat),
            grad_values.reshape(flat),
        ],
        axis=1,
    )
    grad_first = scatter_rows(back_dot(grad_joint, attend_columns))
    attend_block = to_rows(outer_dot(first_all, grad_joint), wide, narrow)
    gain_one = jnp.sum(grad_first * normed_one, axis=0)
    input_grad = grad_middle + norm_back(grad_first * gains[0], normed_one, inverse_one)
    gain_sums = lax.psum_scatter(
        jnp.stack([gain_one, gain_two]), ("wide", "narrow"), scatter_dimension=1, tiled=True
    )
    return (
        layer_output.reshape(tokens.shape),
        input_grad.reshape(tokens.shape),
        gain_sums[0],
        own_rows(attend_block, 0, head_width),
        own_rows(attend_block, head_width, head_width),
        own_rows(attend_block, 2 * head_width, head_width),
        out_grad,
        gain_sums[1],
        gate_grad,
        up_grad,
        down_grad,
    )


def local(wide, narrow, *arrays):
    if arrays[0].shape[2] // HEAD_DIM % wide == 0:
        return split_plan(wide, narrow, *arrays)
    return gathered_plan(*arrays)


def solution(mesh):
    in_specs = (
        P(None, ("wide", "narrow"), None),
        P(None, ("wide", "narrow")),
        P(None, ("wide", "narrow"), None),
        P(("wide", "narrow")),
        P(("wide", "narrow"), None),
        P(("wide", "narrow"), None),
        P(("wide", "narrow"), None),
        P(("wide", "narrow"), None),
        P(("wide", "narrow")),
        P(("wide", "narrow"), None),
        P(("wide", "narrow"), None),
        P(("wide", "narrow"), None),
    )
    out_specs = (
        P(None, ("wide", "narrow"), None),
        P(None, ("wide", "narrow"), None),
        P(("wide", "narrow")),
        P(("wide", "narrow"), None),
        P(("wide", "narrow"), None),
        P(("wide", "narrow"), None),
        P(("wide", "narrow"), None),
        P(("wide", "narrow")),
        P(("wide", "narrow"), None),
        P(("wide", "narrow"), None),
        P(("wide", "narrow"), None),
    )
    body = functools.partial(local, mesh.shape["wide"], mesh.shape["narrow"])
    return jax.shard_map(body, mesh=mesh, in_specs=in_specs, out_specs=out_specs, check_vma=False)
```

```python
import functools
import math

import jax
import jax.numpy as jnp
from jax import lax
from jax.experimental import pallas as pl
from jax.experimental.pallas import tpu as pltpu
from jax.sharding import PartitionSpec as P

HEAD_DIM = 128
MESH = pl.DeviceIdType.MESH
RING_COST = pl.CostEstimate(flops=0, bytes_accessed=150_000_000, transcendentals=0)


epsilon = 1e-05
rope_base = 10000.0


def mixed_dot(left, right):
    return jnp.dot(left, right, preferred_element_type=jnp.float32)


def outer_dot(left, right):
    return lax.dot_general(
        left, right, (((0,), (0,)), ((), ())), preferred_element_type=jnp.float32
    )


def back_dot(left, right):
    return lax.dot_general(
        left, right, (((1,), (1,)), ((), ())), preferred_element_type=jnp.float32
    )


def joined(pieces):
    return jnp.concatenate(pieces, axis=0)


def rotation_tables(length):
    half_size = HEAD_DIM // 2
    position = jnp.arange(length).astype(jnp.float32)
    frequency = rope_base ** (-jnp.arange(half_size).astype(jnp.float32) / half_size)
    angles = position[:, None] * frequency[None, :]
    return (jnp.cos(angles), jnp.sin(angles))


def rotate(values, cosine, sine_table):
    half_size = values.shape[-1] // 2
    front_half = values[..., :half_size]
    back_half = values[..., half_size:]
    cos_wide = cosine[:, None, :]
    sin_wide = sine_table[:, None, :]
    return jnp.concatenate(
        [
            front_half * cos_wide - back_half * sin_wide,
            back_half * cos_wide + front_half * sin_wide,
        ],
        axis=-1,
    )


def norm_back(grad_normed, normed, inverse):
    return inverse * (grad_normed - normed * jnp.mean(grad_normed * normed, axis=-1, keepdims=True))


def score_gates(queries, keys_rot):
    length = queries.shape[0]
    scores = jnp.einsum(
        "qhd,khd->hqk", queries, keys_rot, preferred_element_type=jnp.float32
    ) * HEAD_DIM ** (-0.5) - math.log(length)
    causal = (jnp.arange(length)[:, None] >= jnp.arange(length)[None, :]).astype(jnp.float32)
    return (jax.nn.sigmoid(scores), causal)


def attention_forward(inputs, attend_full):
    norm_gain, query_weight, key_weight, value_weight, out_weight = attend_full
    length, model_width = inputs.shape
    heads_count = model_width // HEAD_DIM
    floats = inputs.astype(jnp.float32)
    inverse = lax.rsqrt(jnp.mean(floats * floats, axis=-1, keepdims=True) + epsilon)
    normed = floats * inverse
    lowered = (normed * norm_gain.astype(jnp.float32)).astype(jnp.bfloat16)
    cosine, sine_table = rotation_tables(length)
    queries = rotate(
        mixed_dot(lowered, query_weight).reshape(length, heads_count, HEAD_DIM), cosine, sine_table
    ).astype(jnp.bfloat16)
    keys_rot = rotate(
        mixed_dot(lowered, key_weight).reshape(length, heads_count, HEAD_DIM), cosine, sine_table
    ).astype(jnp.bfloat16)
    values_all = (
        mixed_dot(lowered, value_weight).astype(jnp.bfloat16).reshape(length, heads_count, HEAD_DIM)
    )
    gates_sig, causal = score_gates(queries, keys_rot)
    weights_low = (gates_sig * causal).astype(jnp.bfloat16)
    attended = jnp.einsum(
        "hqk,khd->qhd", weights_low, values_all, preferred_element_type=jnp.float32
    )
    attended = attended.astype(jnp.bfloat16).reshape(length, model_width)
    middle = floats + mixed_dot(attended, out_weight)
    return (middle, (inverse, normed, lowered, queries, keys_rot, values_all, attended))


def feed_front(middle, front_full):
    norm_gain, gate_weight, up_weight = front_full
    inverse = lax.rsqrt(jnp.mean(middle * middle, axis=-1, keepdims=True) + epsilon)
    normed = middle * inverse
    lowered = (normed * norm_gain.astype(jnp.float32)).astype(jnp.bfloat16)
    gate_value = mixed_dot(lowered, gate_weight)
    up_value = mixed_dot(lowered, up_weight)
    hidden = (jax.nn.silu(gate_value) * up_value).astype(jnp.bfloat16)
    return (hidden, (inverse, normed, lowered, gate_value, up_value, hidden))


def attention_backward(grad_middle, saved_state, attend_full):
    norm_gain, query_weight, key_weight, value_weight, out_weight = attend_full
    inverse, normed, lowered, queries, keys_rot, values_all, attended = saved_state
    length, model_width = grad_middle.shape
    heads_count = model_width // HEAD_DIM
    grad_low = grad_middle.astype(jnp.bfloat16)
    grad_attended = (
        back_dot(grad_low, out_weight).astype(jnp.bfloat16).reshape(length, heads_count, HEAD_DIM)
    )
    gates_sig, causal = score_gates(queries, keys_rot)
    weights_low = (gates_sig * causal).astype(jnp.bfloat16)
    grad_weights = jnp.einsum(
        "qhd,khd->hqk", grad_attended, values_all, preferred_element_type=jnp.float32
    )
    grad_values = jnp.einsum(
        "hqk,qhd->khd", weights_low, grad_attended, preferred_element_type=jnp.float32
    )
    grad_values = grad_values.astype(jnp.bfloat16).reshape(length, model_width)
    grad_scores = (grad_weights * gates_sig * (1.0 - gates_sig) * causal).astype(jnp.bfloat16)
    scale_factor = HEAD_DIM ** (-0.5)
    cosine, sine_table = rotation_tables(length)
    query_rot = (
        jnp.einsum("hqk,khd->qhd", grad_scores, keys_rot, preferred_element_type=jnp.float32)
        * scale_factor
    )
    key_rot = (
        jnp.einsum("hqk,qhd->khd", grad_scores, queries, preferred_element_type=jnp.float32)
        * scale_factor
    )
    grad_queries = (
        rotate(query_rot, cosine, -sine_table).astype(jnp.bfloat16).reshape(length, model_width)
    )
    grad_keys = (
        rotate(key_rot, cosine, -sine_table).astype(jnp.bfloat16).reshape(length, model_width)
    )
    grad_lowered = (
        back_dot(grad_queries, query_weight)
        + back_dot(grad_keys, key_weight)
        + back_dot(grad_values, value_weight)
    )
    gain_term = jnp.sum(grad_lowered * normed, axis=0)
    grad_inputs = grad_middle + norm_back(
        grad_lowered * norm_gain.astype(jnp.float32), normed, inverse
    )
    return (grad_inputs, gain_term, (grad_queries, grad_keys, grad_values, grad_low))


def gathered_plan(
    tokens,
    lengths,
    cotangent,
    norm1_gain,
    query_weight,
    key_weight,
    value_weight,
    out_weight,
    norm2_gain,
    gate_weight,
    up_weight,
    down_weight,
):
    micro_count = tokens.shape[0]
    length = tokens.shape[1]
    position = jnp.arange(length, dtype=jnp.int32)
    row_masks = [
        (position < lengths[micro_index, 0]).astype(jnp.float32)
        for micro_index in range(micro_count)
    ]
    attend_full = (
        lax.all_gather(norm1_gain, ("wide", "narrow"), axis=0, tiled=True),
        lax.all_gather(query_weight, ("wide", "narrow"), axis=0, tiled=True),
        lax.all_gather(key_weight, ("wide", "narrow"), axis=0, tiled=True),
        lax.all_gather(value_weight, ("wide", "narrow"), axis=0, tiled=True),
        lax.all_gather(out_weight, ("wide", "narrow"), axis=0, tiled=True),
    )
    middles = []
    attend_states = []
    for micro_index in range(micro_count):
        middle, attend_state = attention_forward(tokens[micro_index], attend_full)
        middles.append(middle)
        attend_states.append(attend_state)
    front_full = (
        lax.all_gather(norm2_gain, ("wide", "narrow"), axis=0, tiled=True),
        lax.all_gather(gate_weight, ("wide", "narrow"), axis=0, tiled=True),
        lax.all_gather(up_weight, ("wide", "narrow"), axis=0, tiled=True),
    )
    feed_states = []
    for micro_index in range(micro_count):
        hidden, feed_state = feed_front(middles[micro_index], front_full)
        feed_states.append(feed_state)
    down_full = lax.all_gather(down_weight, ("wide", "narrow"), axis=0, tiled=True)
    layer_rows = []
    for micro_index in range(micro_count):
        result = (
            middles[micro_index] + mixed_dot(feed_states[micro_index][5], down_full)
        ) * row_masks[micro_index][:, None]
        layer_rows.append(result.astype(jnp.bfloat16))
    down_back = lax.all_gather(down_weight, ("wide", "narrow"), axis=0, tiled=True)
    upstreams = []
    upstream_lows = []
    grad_gates = []
    grad_ups = []
    for micro_index in range(micro_count):
        inverse, normed, lowered, gate_value, up_value, hidden = feed_states[micro_index]
        upstream = cotangent[micro_index].astype(jnp.float32) * row_masks[micro_index][:, None]
        upstream_low = upstream.astype(jnp.bfloat16)
        grad_hidden = back_dot(upstream_low, down_back)
        gate_sig = jax.nn.sigmoid(gate_value)
        grad_gates.append(
            (grad_hidden * up_value * gate_sig * (1.0 + gate_value * (1.0 - gate_sig))).astype(
                jnp.bfloat16
            )
        )
        grad_ups.append((grad_hidden * gate_value * gate_sig).astype(jnp.bfloat16))
        upstreams.append(upstream)
        upstream_lows.append(upstream_low)
    hidden_rows = joined([state[5] for state in feed_states])
    lowered_rows = joined([state[2] for state in feed_states])
    down_sum = lax.psum_scatter(
        outer_dot(hidden_rows, joined(upstream_lows)),
        ("wide", "narrow"),
        scatter_dimension=0,
        tiled=True,
    )
    gain_two, gate_back = (
        lax.all_gather(norm2_gain, ("wide", "narrow"), axis=0, tiled=True),
        lax.all_gather(gate_weight, ("wide", "narrow"), axis=0, tiled=True),
    )
    grad_loweds = [
        back_dot(grad_gates[micro_index], gate_back) for micro_index in range(micro_count)
    ]
    gate_sum = lax.psum_scatter(
        outer_dot(lowered_rows, joined(grad_gates)),
        ("wide", "narrow"),
        scatter_dimension=0,
        tiled=True,
    )
    up_back = lax.all_gather(up_weight, ("wide", "narrow"), axis=0, tiled=True)
    gain_total = jnp.zeros((tokens.shape[2],), jnp.float32)
    grad_middles = []
    for micro_index in range(micro_count):
        inverse, normed, lowered, gate_value, up_value, hidden = feed_states[micro_index]
        grad_lowered = grad_loweds[micro_index] + back_dot(grad_ups[micro_index], up_back)
        gain_total = gain_total + jnp.sum(grad_lowered * normed, axis=0)
        grad_middles.append(
            upstreams[micro_index]
            + norm_back(grad_lowered * gain_two.astype(jnp.float32), normed, inverse)
        )
    up_total = outer_dot(lowered_rows, joined(grad_ups))
    gain_two_sum, up_sum = (
        lax.psum_scatter(gain_total, ("wide", "narrow"), scatter_dimension=0, tiled=True),
        lax.psum_scatter(up_total, ("wide", "narrow"), scatter_dimension=0, tiled=True),
    )
    attend_back = (
        lax.all_gather(norm1_gain, ("wide", "narrow"), axis=0, tiled=True),
        lax.all_gather(query_weight, ("wide", "narrow"), axis=0, tiled=True),
        lax.all_gather(key_weight, ("wide", "narrow"), axis=0, tiled=True),
        lax.all_gather(value_weight, ("wide", "narrow"), axis=0, tiled=True),
        lax.all_gather(out_weight, ("wide", "narrow"), axis=0, tiled=True),
    )
    input_rows = []
    gain_first = jnp.zeros((tokens.shape[2],), jnp.float32)
    grad_lists = ([], [], [], [])
    for micro_index in range(micro_count):
        grad_inputs, gain_term, row_grads = attention_backward(
            grad_middles[micro_index], attend_states[micro_index], attend_back
        )
        input_rows.append(grad_inputs)
        gain_first = gain_first + gain_term
        for slot_index in range(4):
            grad_lists[slot_index].append(row_grads[slot_index])
    first_rows = joined([state[2] for state in attend_states])
    attended_rows = joined([state[6] for state in attend_states])
    query_total = outer_dot(first_rows, joined(grad_lists[0]))
    key_total = outer_dot(first_rows, joined(grad_lists[1]))
    value_total = outer_dot(first_rows, joined(grad_lists[2]))
    out_total = outer_dot(attended_rows, joined(grad_lists[3]))
    attend_sums = (
        lax.psum_scatter(gain_first, ("wide", "narrow"), scatter_dimension=0, tiled=True),
        lax.psum_scatter(query_total, ("wide", "narrow"), scatter_dimension=0, tiled=True),
        lax.psum_scatter(key_total, ("wide", "narrow"), scatter_dimension=0, tiled=True),
        lax.psum_scatter(value_total, ("wide", "narrow"), scatter_dimension=0, tiled=True),
        lax.psum_scatter(out_total, ("wide", "narrow"), scatter_dimension=0, tiled=True),
    )
    layer_output = jnp.stack(layer_rows)
    input_grad = jnp.stack(input_rows)
    return (
        layer_output,
        input_grad,
        attend_sums[0],
        attend_sums[1],
        attend_sums[2],
        attend_sums[3],
        attend_sums[4],
        gain_two_sum,
        gate_sum,
        up_sum,
        down_sum,
    )


def ring_place(device, size):
    height, side = device // 2, device % 2
    return height * (1 - side) + (size - 1 - height) * side


def ring_device(place, size):
    back = place // (size // 2)
    return (1 - back) * 2 * place + back * (2 * (size - 1 - place) + 1)


def enter_ring(left, right):
    barrier = pltpu.get_barrier_semaphore()
    for device in (left, right):
        pl.semaphore_signal(barrier, inc=1, device_id={"wide": device}, device_id_type=MESH)
    pl.semaphore_wait(barrier, 2)


def gather_kernel(size, block_ref, full_ref, own_sem, send_sem, recv_sem):
    place = ring_place(lax.axis_index("wide"), size)
    left = ring_device((place + size - 1) % size, size)
    right = ring_device((place + 1) % size, size)
    half = block_ref.shape[0] // 2
    hops = size // 2

    def copy(way, hop, part):
        origin = ring_device((place + size - hop if way == 0 else place + hop) % size, size)
        target = full_ref.at[origin, pl.ds(part * half, half)]
        source = block_ref.at[pl.ds(part * half, half)] if hop == 0 else target
        return pltpu.make_async_remote_copy(
            src_ref=source,
            dst_ref=target,
            send_sem=send_sem.at[way, hop, part],
            recv_sem=recv_sem.at[way, hop, part],
            device_id={"wide": right if way == 0 else left},
            device_id_type=MESH,
        )

    enter_ring(left, right)
    own = pltpu.make_async_copy(block_ref, full_ref.at[lax.axis_index("wide")], own_sem)
    sent = {}
    for hop in range(hops):
        for part in range(2):
            for way in range(2):
                if hop == hops - 1 and part != way:
                    continue
                if hop:
                    sent[way, hop - 1, part].wait_recv()
                sent[way, hop, part] = copy(way, hop, part)
                sent[way, hop, part].start()
        if hop == 0:
            own.start()
    for way in range(2):
        sent[way, hops - 2, 1 - way].wait_recv()
        sent[way, hops - 1, way].wait_recv()
    for transfer in sent.values():
        transfer.wait_send()
    own.wait()


def gather_rows(block, size):
    rows, width = block.shape
    hops = size // 2
    full = pl.pallas_call(
        functools.partial(gather_kernel, size),
        out_shape=jax.ShapeDtypeStruct((size, rows, width), block.dtype),
        in_specs=[pl.BlockSpec(memory_space=pltpu.VMEM)],
        out_specs=pl.BlockSpec(memory_space=pl.ANY),
        scratch_shapes=[
            pltpu.SemaphoreType.DMA,
            pltpu.SemaphoreType.DMA((2, hops, 2)),
            pltpu.SemaphoreType.DMA((2, hops, 2)),
        ],
        compiler_params=pltpu.CompilerParams(collective_id=0, has_side_effects=True),
        cost_estimate=RING_COST,
        name="gather_rows",
    )(block)
    return full.reshape(size * rows, width)


def scatter_kernel(size, partial_ref, sum_ref, held, send_sem, recv_sem):
    place = ring_place(lax.axis_index("wide"), size)
    left = ring_device((place + size - 1) % size, size)
    right = ring_device((place + 1) % size, size)
    rows, width = sum_ref.shape
    rows, width = rows // 2, width // 2

    def cut(way, part):
        return pl.ds(part * rows, rows), pl.ds(way * width, width)

    def mine(way, hop, part):
        block = ring_device((place + 2 * size - 1 - hop if way == 0 else place + 1 + hop) % size, size)
        return partial_ref.at[(block, *cut(way, part))]

    def copy(way, hop, part):
        source = mine(way, hop, part) if hop == 0 else held.at[(hop - 1, *cut(way, part))]
        return pltpu.make_async_remote_copy(
            src_ref=source,
            dst_ref=held.at[(hop, *cut(way, part))],
            send_sem=send_sem.at[way, hop, part],
            recv_sem=recv_sem.at[way, hop, part],
            device_id={"wide": right if way == 0 else left},
            device_id_type=MESH,
        )

    enter_ring(left, right)
    sent = {}
    for hop in range(size):
        for part in range(2):
            for way in range(2):
                if hop:
                    sent[way, hop - 1, part].wait_recv()
                    arrived = held.at[(hop - 1, *cut(way, part))]
                    total = arrived[...].astype(jnp.float32) + mine(way, hop, part)[...].astype(
                        jnp.float32
                    )
                    if hop == size - 1:
                        sum_ref[cut(way, part)] = total
                        continue
                    arrived[...] = total.astype(jnp.bfloat16)
                sent[way, hop, part] = copy(way, hop, part)
                sent[way, hop, part].start()
    for transfer in sent.values():
        transfer.wait_send()


def scatter_rows(partial, size):
    rows, width = partial.shape[0] // size, partial.shape[1]
    steps = size - 1
    return pl.pallas_call(
        functools.partial(scatter_kernel, size),
        out_shape=jax.ShapeDtypeStruct((rows, width), jnp.float32),
        in_specs=[pl.BlockSpec(memory_space=pltpu.VMEM)],
        out_specs=pl.BlockSpec(memory_space=pltpu.VMEM),
        scratch_shapes=[
            pltpu.VMEM((steps, rows, width), jnp.bfloat16),
            pltpu.SemaphoreType.DMA((2, steps, 2)),
            pltpu.SemaphoreType.DMA((2, steps, 2)),
        ],
        compiler_params=pltpu.CompilerParams(collective_id=1, has_side_effects=True),
        cost_estimate=RING_COST,
        name="scatter_rows",
    )(partial.astype(jnp.bfloat16).reshape(size, rows, width))


def to_columns(weights, wide):
    pieces = [w.reshape(w.shape[0], wide, w.shape[1] // wide) for w in weights]
    block = jnp.swapaxes(jnp.concatenate(pieces, axis=2), 0, 1)
    block = lax.all_to_all(block, "wide", split_axis=0, concat_axis=0, tiled=True)
    full = lax.all_gather(block, "narrow", axis=1, tiled=True)
    return full.reshape(-1, full.shape[2])


def to_rows(columns, wide, narrow):
    rows, width = columns.shape
    block = columns.astype(jnp.bfloat16).reshape(wide, rows // wide, width)
    block = lax.psum_scatter(block, "narrow", scatter_dimension=1, tiled=True)
    return lax.all_to_all(block, "wide", split_axis=0, concat_axis=0, tiled=True)


def own_rows(block, start, width):
    piece = block[:, :, start : start + width]
    return jnp.swapaxes(piece, 0, 1).reshape(piece.shape[1], -1).astype(jnp.float32)


def gather_narrow(weight):
    return lax.all_gather(weight, "narrow", axis=0, tiled=True)


def sum_narrow(partial):
    return lax.psum_scatter(
        partial.astype(jnp.bfloat16), "narrow", scatter_dimension=0, tiled=True
    ).astype(jnp.float32)


def rotate_heads(values, cosine, sine_table):
    half_size = HEAD_DIM // 2
    front_half = values[..., :half_size]
    back_half = values[..., half_size:]
    return jnp.concatenate(
        [
            front_half * cosine - back_half * sine_table,
            back_half * cosine + front_half * sine_table,
        ],
        axis=-1,
    )


def split_plan(
    wide,
    narrow,
    tokens,
    lengths,
    cotangent,
    norm1_gain,
    query_weight,
    key_weight,
    value_weight,
    out_weight,
    norm2_gain,
    gate_weight,
    up_weight,
    down_weight,
):
    micro_count, length, width = tokens.shape
    rows = micro_count * length
    sequences = wide * micro_count
    heads = width // HEAD_DIM // wide
    head_width = heads * HEAD_DIM
    hidden_width = gate_weight.shape[1] // wide
    position = jnp.arange(length, dtype=jnp.int32)
    row_mask = (position[None, :] < lengths).astype(jnp.float32).reshape(rows, 1)

    share = norm1_gain.shape[0]
    gains = lax.all_gather(jnp.concatenate([norm1_gain, norm2_gain]), ("wide", "narrow"))
    gains = gains.astype(jnp.float32)
    gains = (gains[:, :share].reshape(width), gains[:, share:].reshape(width))
    attend_columns = to_columns((query_weight, key_weight, value_weight), wide)

    floats = tokens.reshape(rows, width).astype(jnp.float32)
    inverse_one = lax.rsqrt(jnp.mean(floats * floats, axis=-1, keepdims=True) + epsilon)
    normed_one = floats * inverse_one
    floats_all = gather_rows(tokens.reshape(rows, width), wide).astype(jnp.float32)
    inverse_all = lax.rsqrt(jnp.mean(floats_all * floats_all, axis=-1, keepdims=True) + epsilon)
    first_all = (floats_all * inverse_all * gains[0]).astype(jnp.bfloat16)
    feed_columns = to_columns((gate_weight, up_weight), wide)
    out_rows = gather_narrow(out_weight)
    down_rows = gather_narrow(down_weight)

    cosine, sine_table = rotation_tables(length)
    cosine, sine_table = cosine[None, :, None, :], sine_table[None, :, None, :]
    joint = mixed_dot(first_all, attend_columns)
    by_head = (sequences, length, heads, HEAD_DIM)
    queries = rotate_heads(joint[:, :head_width].reshape(by_head), cosine, sine_table).astype(
        jnp.bfloat16
    )
    keys_rot = rotate_heads(
        joint[:, head_width : 2 * head_width].reshape(by_head), cosine, sine_table
    ).astype(jnp.bfloat16)
    values_all = joint[:, 2 * head_width :].reshape(by_head).astype(jnp.bfloat16)
    scores = jnp.einsum(
        "sqhd,skhd->shqk", queries, keys_rot, preferred_element_type=jnp.float32
    ) * HEAD_DIM ** (-0.5) - math.log(length)
    causal = (position[:, None] >= position[None, :]).astype(jnp.float32)
    gates_sig = jax.nn.sigmoid(scores)
    weights_low = (gates_sig * causal).astype(jnp.bfloat16)
    attended = (
        jnp.einsum("shqk,skhd->sqhd", weights_low, values_all, preferred_element_type=jnp.float32)
        .astype(jnp.bfloat16)
        .reshape(sequences * length, head_width)
    )
    middle = floats + scatter_rows(mixed_dot(attended, out_rows), wide)

    inverse_two = lax.rsqrt(jnp.mean(middle * middle, axis=-1, keepdims=True) + epsilon)
    normed_two = middle * inverse_two
    second_all = gather_rows((normed_two * gains[1]).astype(jnp.bfloat16), wide)
    upstream = cotangent.reshape(rows, width).astype(jnp.float32) * row_mask
    upstream_all = gather_rows(upstream.astype(jnp.bfloat16), wide)

    front = mixed_dot(second_all, feed_columns)
    gate_value = front[:, :hidden_width]
    up_value = front[:, hidden_width:]
    gate_sig = jax.nn.sigmoid(gate_value)
    hidden = (gate_value * gate_sig * up_value).astype(jnp.bfloat16)
    feed_out = scatter_rows(mixed_dot(hidden, down_rows), wide)
    layer_output = ((middle + feed_out) * row_mask).astype(jnp.bfloat16)

    grad_hidden = back_dot(upstream_all, down_rows)
    grad_gate = (
        grad_hidden * up_value * gate_sig * (1.0 + gate_value * (1.0 - gate_sig))
    ).astype(jnp.bfloat16)
    grad_up = (grad_hidden * gate_value * gate_sig).astype(jnp.bfloat16)
    grad_front = jnp.concatenate([grad_gate, grad_up], axis=1)
    grad_second = scatter_rows(back_dot(grad_front, feed_columns), wide)
    down_grad = sum_narrow(outer_dot(hidden, upstream_all))
    front_block = to_rows(outer_dot(second_all, grad_front), wide, narrow)
    gate_grad = own_rows(front_block, 0, hidden_width)
    up_grad = own_rows(front_block, hidden_width, hidden_width)

    gain_two = jnp.sum(grad_second * normed_two, axis=0)
    grad_middle = upstream + norm_back(grad_second * gains[1], normed_two, inverse_two)
    middle_all = gather_rows(grad_middle.astype(jnp.bfloat16), wide)

    grad_attended = back_dot(middle_all, out_rows).astype(jnp.bfloat16).reshape(by_head)
    out_grad = sum_narrow(outer_dot(attended, middle_all))
    grad_weights = jnp.einsum(
        "sqhd,skhd->shqk", grad_attended, values_all, preferred_element_type=jnp.float32
    )
    grad_values = jnp.einsum(
        "shqk,sqhd->skhd", weights_low, grad_attended, preferred_element_type=jnp.float32
    ).astype(jnp.bfloat16)
    grad_scores = (grad_weights * gates_sig * (1.0 - gates_sig) * causal).astype(jnp.bfloat16)
    scale_factor = HEAD_DIM ** (-0.5)
    query_rot = (
        jnp.einsum("shqk,skhd->sqhd", grad_scores, keys_rot, preferred_element_type=jnp.float32)
        * scale_factor
    )
    key_rot = (
        jnp.einsum("shqk,sqhd->skhd", grad_scores, queries, preferred_element_type=jnp.float32)
        * scale_factor
    )
    flat = (sequences * length, head_width)
    grad_joint = jnp.concatenate(
        [
            rotate_heads(query_rot, cosine, -sine_table).astype(jnp.bfloat16).reshape(flat),
            rotate_heads(key_rot, cosine, -sine_table).astype(jnp.bfloat16).reshape(flat),
            grad_values.reshape(flat),
        ],
        axis=1,
    )
    grad_first = scatter_rows(back_dot(grad_joint, attend_columns), wide)
    attend_block = to_rows(outer_dot(first_all, grad_joint), wide, narrow)
    gain_one = jnp.sum(grad_first * normed_one, axis=0)
    input_grad = grad_middle + norm_back(grad_first * gains[0], normed_one, inverse_one)
    gain_terms = jnp.concatenate([gain_one.reshape(-1, share), gain_two.reshape(-1, share)], axis=1)
    gain_terms = lax.all_to_all(
        gain_terms, ("wide", "narrow"), split_axis=0, concat_axis=0, tiled=True
    )
    gain_sums = jnp.sum(gain_terms, axis=0)
    return (
        layer_output.reshape(tokens.shape),
        input_grad.reshape(tokens.shape),
        gain_sums[:share],
        own_rows(attend_block, 0, head_width),
        own_rows(attend_block, head_width, head_width),
        own_rows(attend_block, 2 * head_width, head_width),
        out_grad,
        gain_sums[share:],
        gate_grad,
        up_grad,
        down_grad,
    )


def local(wide, narrow, *arrays):
    if arrays[0].shape[2] // HEAD_DIM % wide == 0:
        return split_plan(wide, narrow, *arrays)
    return gathered_plan(*arrays)


def solution(mesh):
    in_specs = (
        P(None, ("wide", "narrow"), None),
        P(None, ("wide", "narrow")),
        P(None, ("wide", "narrow"), None),
        P(("wide", "narrow")),
        P(("wide", "narrow"), None),
        P(("wide", "narrow"), None),
        P(("wide", "narrow"), None),
        P(("wide", "narrow"), None),
        P(("wide", "narrow")),
        P(("wide", "narrow"), None),
        P(("wide", "narrow"), None),
        P(("wide", "narrow"), None),
    )
    out_specs = (
        P(None, ("wide", "narrow"), None),
        P(None, ("wide", "narrow"), None),
        P(("wide", "narrow")),
        P(("wide", "narrow"), None),
        P(("wide", "narrow"), None),
        P(("wide", "narrow"), None),
        P(("wide", "narrow"), None),
        P(("wide", "narrow")),
        P(("wide", "narrow"), None),
        P(("wide", "narrow"), None),
        P(("wide", "narrow"), None),
    )
    body = functools.partial(local, mesh.shape["wide"], mesh.shape["narrow"])
    return jax.shard_map(body, mesh=mesh, in_specs=in_specs, out_specs=out_specs, check_vma=False)
```

```python
import functools
import math

import jax
import jax.numpy as jnp
from jax import lax
from jax.experimental import pallas as pl
from jax.experimental.pallas import tpu as pltpu
from jax.sharding import PartitionSpec as P


HEAD_DIM = 128
AXES = ("wide", "narrow")
WIDE, NARROW = AXES
MESH = pl.DeviceIdType.MESH
RING_COST = pl.CostEstimate(flops=0, bytes_accessed=150_000_000, transcendentals=0)


epsilon = 1e-05
rope_base = 10000.0


def mixed_dot(left, right):
    return jnp.dot(left, right, preferred_element_type=jnp.float32)


def outer_dot(left, right):
    return lax.dot_general(
        left, right, (((0,), (0,)), ((), ())), preferred_element_type=jnp.float32
    )


def back_dot(left, right):
    return lax.dot_general(
        left, right, (((1,), (1,)), ((), ())), preferred_element_type=jnp.float32
    )


def joined(pieces):
    return jnp.concatenate(pieces, axis=0)


def rotation_tables(length):
    half_size = HEAD_DIM // 2
    position = jnp.arange(length).astype(jnp.float32)
    frequency = rope_base ** (-jnp.arange(half_size).astype(jnp.float32) / half_size)
    angles = position[:, None] * frequency[None, :]
    return (jnp.cos(angles), jnp.sin(angles))


def rotate(values, cosine, sine_table):
    half_size = values.shape[-1] // 2
    front_half = values[..., :half_size]
    back_half = values[..., half_size:]
    cos_wide = cosine[:, None, :]
    sin_wide = sine_table[:, None, :]
    return jnp.concatenate(
        [
            front_half * cos_wide - back_half * sin_wide,
            back_half * cos_wide + front_half * sin_wide,
        ],
        axis=-1,
    )


def norm_back(grad_normed, normed, inverse):
    return inverse * (grad_normed - normed * jnp.mean(grad_normed * normed, axis=-1, keepdims=True))


def score_gates(queries, keys_rot):
    length = queries.shape[0]
    scores = jnp.einsum(
        "qhd,khd->hqk", queries, keys_rot, preferred_element_type=jnp.float32
    ) * HEAD_DIM ** (-0.5) - math.log(length)
    causal = (jnp.arange(length)[:, None] >= jnp.arange(length)[None, :]).astype(jnp.float32)
    return (jax.nn.sigmoid(scores), causal)


def attention_forward(inputs, attend_full):
    norm_gain, query_weight, key_weight, value_weight, out_weight = attend_full
    length, model_width = inputs.shape
    heads_count = model_width // HEAD_DIM
    floats = inputs.astype(jnp.float32)
    inverse = lax.rsqrt(jnp.mean(floats * floats, axis=-1, keepdims=True) + epsilon)
    normed = floats * inverse
    lowered = (normed * norm_gain.astype(jnp.float32)).astype(jnp.bfloat16)
    cosine, sine_table = rotation_tables(length)
    queries = rotate(
        mixed_dot(lowered, query_weight).reshape(length, heads_count, HEAD_DIM), cosine, sine_table
    ).astype(jnp.bfloat16)
    keys_rot = rotate(
        mixed_dot(lowered, key_weight).reshape(length, heads_count, HEAD_DIM), cosine, sine_table
    ).astype(jnp.bfloat16)
    values_all = (
        mixed_dot(lowered, value_weight).astype(jnp.bfloat16).reshape(length, heads_count, HEAD_DIM)
    )
    gates_sig, causal = score_gates(queries, keys_rot)
    weights_low = (gates_sig * causal).astype(jnp.bfloat16)
    attended = jnp.einsum(
        "hqk,khd->qhd", weights_low, values_all, preferred_element_type=jnp.float32
    )
    attended = attended.astype(jnp.bfloat16).reshape(length, model_width)
    middle = floats + mixed_dot(attended, out_weight)
    return (middle, (inverse, normed, lowered, queries, keys_rot, values_all, attended))


def feed_front(middle, front_full):
    norm_gain, gate_weight, up_weight = front_full
    inverse = lax.rsqrt(jnp.mean(middle * middle, axis=-1, keepdims=True) + epsilon)
    normed = middle * inverse
    lowered = (normed * norm_gain.astype(jnp.float32)).astype(jnp.bfloat16)
    gate_value = mixed_dot(lowered, gate_weight)
    up_value = mixed_dot(lowered, up_weight)
    hidden = (jax.nn.silu(gate_value) * up_value).astype(jnp.bfloat16)
    return (hidden, (inverse, normed, lowered, gate_value, up_value, hidden))


def attention_backward(grad_middle, saved_state, attend_full):
    norm_gain, query_weight, key_weight, value_weight, out_weight = attend_full
    inverse, normed, _, queries, keys_rot, values_all, _ = saved_state
    length, model_width = grad_middle.shape
    heads_count = model_width // HEAD_DIM
    grad_low = grad_middle.astype(jnp.bfloat16)
    grad_attended = (
        back_dot(grad_low, out_weight).astype(jnp.bfloat16).reshape(length, heads_count, HEAD_DIM)
    )
    gates_sig, causal = score_gates(queries, keys_rot)
    weights_low = (gates_sig * causal).astype(jnp.bfloat16)
    grad_weights = jnp.einsum(
        "qhd,khd->hqk", grad_attended, values_all, preferred_element_type=jnp.float32
    )
    grad_values = jnp.einsum(
        "hqk,qhd->khd", weights_low, grad_attended, preferred_element_type=jnp.float32
    )
    grad_values = grad_values.astype(jnp.bfloat16).reshape(length, model_width)
    grad_scores = (grad_weights * gates_sig * (1.0 - gates_sig) * causal).astype(jnp.bfloat16)
    scale_factor = HEAD_DIM ** (-0.5)
    cosine, sine_table = rotation_tables(length)
    query_rot = (
        jnp.einsum("hqk,khd->qhd", grad_scores, keys_rot, preferred_element_type=jnp.float32)
        * scale_factor
    )
    key_rot = (
        jnp.einsum("hqk,qhd->khd", grad_scores, queries, preferred_element_type=jnp.float32)
        * scale_factor
    )
    grad_queries = (
        rotate(query_rot, cosine, -sine_table).astype(jnp.bfloat16).reshape(length, model_width)
    )
    grad_keys = (
        rotate(key_rot, cosine, -sine_table).astype(jnp.bfloat16).reshape(length, model_width)
    )
    grad_lowered = (
        back_dot(grad_queries, query_weight)
        + back_dot(grad_keys, key_weight)
        + back_dot(grad_values, value_weight)
    )
    gain_term = jnp.sum(grad_lowered * normed, axis=0)
    grad_inputs = grad_middle + norm_back(
        grad_lowered * norm_gain.astype(jnp.float32), normed, inverse
    )
    return (grad_inputs, gain_term, (grad_queries, grad_keys, grad_values, grad_low))


def gathered_plan(
    tokens,
    lengths,
    cotangent,
    norm1_gain,
    query_weight,
    key_weight,
    value_weight,
    out_weight,
    norm2_gain,
    gate_weight,
    up_weight,
    down_weight,
):
    micro_count = tokens.shape[0]
    length = tokens.shape[1]
    position = jnp.arange(length, dtype=jnp.int32)
    row_masks = [
        (position < lengths[micro_index, 0]).astype(jnp.float32)
        for micro_index in range(micro_count)
    ]
    attend_full = (
        lax.all_gather(norm1_gain, AXES, axis=0, tiled=True),
        lax.all_gather(query_weight, AXES, axis=0, tiled=True),
        lax.all_gather(key_weight, AXES, axis=0, tiled=True),
        lax.all_gather(value_weight, AXES, axis=0, tiled=True),
        lax.all_gather(out_weight, AXES, axis=0, tiled=True),
    )
    middles = []
    attend_states = []
    for micro_index in range(micro_count):
        middle, attend_state = attention_forward(tokens[micro_index], attend_full)
        middles.append(middle)
        attend_states.append(attend_state)
    front_full = (
        lax.all_gather(norm2_gain, AXES, axis=0, tiled=True),
        lax.all_gather(gate_weight, AXES, axis=0, tiled=True),
        lax.all_gather(up_weight, AXES, axis=0, tiled=True),
    )
    feed_states = []
    for micro_index in range(micro_count):
        hidden, feed_state = feed_front(middles[micro_index], front_full)
        feed_states.append(feed_state)
    down_full = lax.all_gather(down_weight, AXES, axis=0, tiled=True)
    layer_rows = []
    for micro_index in range(micro_count):
        result = (
            middles[micro_index] + mixed_dot(feed_states[micro_index][5], down_full)
        ) * row_masks[micro_index][:, None]
        layer_rows.append(result.astype(jnp.bfloat16))
    down_back = lax.all_gather(down_weight, AXES, axis=0, tiled=True)
    upstreams = []
    upstream_lows = []
    grad_gates = []
    grad_ups = []
    for micro_index in range(micro_count):
        inverse, normed, lowered, gate_value, up_value, hidden = feed_states[micro_index]
        upstream = cotangent[micro_index].astype(jnp.float32) * row_masks[micro_index][:, None]
        upstream_low = upstream.astype(jnp.bfloat16)
        grad_hidden = back_dot(upstream_low, down_back)
        gate_sig = jax.nn.sigmoid(gate_value)
        grad_gates.append(
            (grad_hidden * up_value * gate_sig * (1.0 + gate_value * (1.0 - gate_sig))).astype(
                jnp.bfloat16
            )
        )
        grad_ups.append((grad_hidden * gate_value * gate_sig).astype(jnp.bfloat16))
        upstreams.append(upstream)
        upstream_lows.append(upstream_low)
    hidden_rows = joined([state[5] for state in feed_states])
    lowered_rows = joined([state[2] for state in feed_states])
    down_sum = lax.psum_scatter(
        outer_dot(hidden_rows, joined(upstream_lows)),
        AXES,
        scatter_dimension=0,
        tiled=True,
    )
    gain_two, gate_back = (
        lax.all_gather(norm2_gain, AXES, axis=0, tiled=True),
        lax.all_gather(gate_weight, AXES, axis=0, tiled=True),
    )
    grad_loweds = [
        back_dot(grad_gates[micro_index], gate_back) for micro_index in range(micro_count)
    ]
    gate_sum = lax.psum_scatter(
        outer_dot(lowered_rows, joined(grad_gates)),
        AXES,
        scatter_dimension=0,
        tiled=True,
    )
    up_back = lax.all_gather(up_weight, AXES, axis=0, tiled=True)
    gain_total = jnp.zeros((tokens.shape[2],), jnp.float32)
    grad_middles = []
    for micro_index in range(micro_count):
        inverse, normed, lowered, gate_value, up_value, hidden = feed_states[micro_index]
        grad_lowered = grad_loweds[micro_index] + back_dot(grad_ups[micro_index], up_back)
        gain_total = gain_total + jnp.sum(grad_lowered * normed, axis=0)
        grad_middles.append(
            upstreams[micro_index]
            + norm_back(grad_lowered * gain_two.astype(jnp.float32), normed, inverse)
        )
    up_total = outer_dot(lowered_rows, joined(grad_ups))
    gain_two_sum, up_sum = (
        lax.psum_scatter(gain_total, AXES, scatter_dimension=0, tiled=True),
        lax.psum_scatter(up_total, AXES, scatter_dimension=0, tiled=True),
    )
    attend_back = (
        lax.all_gather(norm1_gain, AXES, axis=0, tiled=True),
        lax.all_gather(query_weight, AXES, axis=0, tiled=True),
        lax.all_gather(key_weight, AXES, axis=0, tiled=True),
        lax.all_gather(value_weight, AXES, axis=0, tiled=True),
        lax.all_gather(out_weight, AXES, axis=0, tiled=True),
    )
    input_rows = []
    gain_first = jnp.zeros((tokens.shape[2],), jnp.float32)
    grad_lists = ([], [], [], [])
    for micro_index in range(micro_count):
        grad_inputs, gain_term, row_grads = attention_backward(
            grad_middles[micro_index], attend_states[micro_index], attend_back
        )
        input_rows.append(grad_inputs)
        gain_first = gain_first + gain_term
        for slot_index in range(4):
            grad_lists[slot_index].append(row_grads[slot_index])
    first_rows = joined([state[2] for state in attend_states])
    attended_rows = joined([state[6] for state in attend_states])
    query_total = outer_dot(first_rows, joined(grad_lists[0]))
    key_total = outer_dot(first_rows, joined(grad_lists[1]))
    value_total = outer_dot(first_rows, joined(grad_lists[2]))
    out_total = outer_dot(attended_rows, joined(grad_lists[3]))
    attend_sums = (
        lax.psum_scatter(gain_first, AXES, scatter_dimension=0, tiled=True),
        lax.psum_scatter(query_total, AXES, scatter_dimension=0, tiled=True),
        lax.psum_scatter(key_total, AXES, scatter_dimension=0, tiled=True),
        lax.psum_scatter(value_total, AXES, scatter_dimension=0, tiled=True),
        lax.psum_scatter(out_total, AXES, scatter_dimension=0, tiled=True),
    )
    layer_output = jnp.stack(layer_rows)
    input_grad = jnp.stack(input_rows)
    return (
        layer_output,
        input_grad,
        attend_sums[0],
        attend_sums[1],
        attend_sums[2],
        attend_sums[3],
        attend_sums[4],
        gain_two_sum,
        gate_sum,
        up_sum,
        down_sum,
    )


def ring_place(device, size):
    height, side = device // 2, device % 2
    return height * (1 - side) + (size - 1 - height) * side


def ring_device(place, size):
    back = place // (size // 2)
    return (1 - back) * 2 * place + back * (2 * (size - 1 - place) + 1)


def enter_ring(left, right):
    barrier = pltpu.get_barrier_semaphore()
    for device in (left, right):
        pl.semaphore_signal(barrier, inc=1, device_id={WIDE: device}, device_id_type=MESH)
    pl.semaphore_wait(barrier, 2)


def gather_kernel(size, block_ref, full_ref, own_sem, send_sem, recv_sem):
    place = ring_place(lax.axis_index(WIDE), size)
    left = ring_device((place + size - 1) % size, size)
    right = ring_device((place + 1) % size, size)
    half = block_ref.shape[0] // 2
    hops = size // 2

    def copy(way, hop, part):
        origin = ring_device((place + size - hop if way == 0 else place + hop) % size, size)
        target = full_ref.at[origin, pl.ds(part * half, half)]
        source = block_ref.at[pl.ds(part * half, half)] if hop == 0 else target
        return pltpu.make_async_remote_copy(
            src_ref=source,
            dst_ref=target,
            send_sem=send_sem.at[way, hop, part],
            recv_sem=recv_sem.at[way, hop, part],
            device_id={WIDE: right if way == 0 else left},
            device_id_type=MESH,
        )

    enter_ring(left, right)
    own = pltpu.make_async_copy(block_ref, full_ref.at[lax.axis_index(WIDE)], own_sem)
    sent = {}
    for hop in range(hops):
        for part in range(2):
            for way in range(2):
                if hop == hops - 1 and part != way:
                    continue
                if hop:
                    sent[way, hop - 1, part].wait_recv()
                sent[way, hop, part] = copy(way, hop, part)
                sent[way, hop, part].start()
        if hop == 0:
            own.start()
    for way in range(2):
        sent[way, hops - 2, 1 - way].wait_recv()
        sent[way, hops - 1, way].wait_recv()
    for transfer in sent.values():
        transfer.wait_send()
    own.wait()


def gather_rows(block, size):
    rows, width = block.shape
    hops = size // 2
    full = pl.pallas_call(
        functools.partial(gather_kernel, size),
        out_shape=jax.ShapeDtypeStruct((size, rows, width), block.dtype),
        in_specs=[pl.BlockSpec(memory_space=pltpu.VMEM)],
        out_specs=pl.BlockSpec(memory_space=pl.ANY),
        scratch_shapes=[
            pltpu.SemaphoreType.DMA,
            pltpu.SemaphoreType.DMA((2, hops, 2)),
            pltpu.SemaphoreType.DMA((2, hops, 2)),
        ],
        compiler_params=pltpu.CompilerParams(collective_id=0, has_side_effects=True),
        cost_estimate=RING_COST,
        name="gather_rows",
    )(block)
    return full.reshape(size * rows, width)


def scatter_kernel(size, partial_ref, sum_ref, held, send_sem, recv_sem):
    place = ring_place(lax.axis_index(WIDE), size)
    left = ring_device((place + size - 1) % size, size)
    right = ring_device((place + 1) % size, size)
    rows, width = sum_ref.shape
    rows, width = rows // 2, width // 2

    def cut(way, part):
        return pl.ds(part * rows, rows), pl.ds(way * width, width)

    def mine(way, hop, part):
        block = ring_device((place + 2 * size - 1 - hop if way == 0 else place + 1 + hop) % size, size)
        return partial_ref.at[(block, *cut(way, part))]

    def copy(way, hop, part):
        source = mine(way, hop, part) if hop == 0 else held.at[(hop - 1, *cut(way, part))]
        return pltpu.make_async_remote_copy(
            src_ref=source,
            dst_ref=held.at[(hop, *cut(way, part))],
            send_sem=send_sem.at[way, hop, part],
            recv_sem=recv_sem.at[way, hop, part],
            device_id={WIDE: right if way == 0 else left},
            device_id_type=MESH,
        )

    enter_ring(left, right)
    sent = {}
    for hop in range(size):
        for part in range(2):
            for way in range(2):
                if hop:
                    sent[way, hop - 1, part].wait_recv()
                    arrived = held.at[(hop - 1, *cut(way, part))]
                    total = arrived[...].astype(jnp.float32) + mine(way, hop, part)[...].astype(
                        jnp.float32
                    )
                    if hop == size - 1:
                        sum_ref[cut(way, part)] = total
                        continue
                    arrived[...] = total.astype(jnp.bfloat16)
                sent[way, hop, part] = copy(way, hop, part)
                sent[way, hop, part].start()
    for transfer in sent.values():
        transfer.wait_send()


def scatter_rows(partial, size):
    rows, width = partial.shape[0] // size, partial.shape[1]
    steps = size - 1
    return pl.pallas_call(
        functools.partial(scatter_kernel, size),
        out_shape=jax.ShapeDtypeStruct((rows, width), jnp.float32),
        in_specs=[pl.BlockSpec(memory_space=pltpu.VMEM)],
        out_specs=pl.BlockSpec(memory_space=pltpu.VMEM),
        scratch_shapes=[
            pltpu.VMEM((steps, rows, width), jnp.bfloat16),
            pltpu.SemaphoreType.DMA((2, steps, 2)),
            pltpu.SemaphoreType.DMA((2, steps, 2)),
        ],
        compiler_params=pltpu.CompilerParams(collective_id=1, has_side_effects=True),
        cost_estimate=RING_COST,
        name="scatter_rows",
    )(partial.astype(jnp.bfloat16).reshape(size, rows, width))


def by_column(weights, wide):
    pieces = [w.reshape(w.shape[0], wide, w.shape[1] // wide) for w in weights]
    return jnp.swapaxes(jnp.concatenate(pieces, axis=2), 0, 1)


def to_columns(block):
    block = lax.all_to_all(block, WIDE, split_axis=0, concat_axis=0, tiled=True)
    full = lax.all_gather(block, NARROW, axis=1, tiled=True)
    return full.reshape(-1, full.shape[2])


def sum_blocks(columns, wide):
    rows, width = columns.shape
    block = columns.astype(jnp.bfloat16).reshape(wide, rows // wide, width)
    return lax.psum_scatter(block, NARROW, scatter_dimension=1, tiled=True)


def to_rows(block):
    return lax.all_to_all(block, WIDE, split_axis=0, concat_axis=0, tiled=True)


def own_rows(block, start, width):
    piece = block[:, :, start : start + width]
    return jnp.swapaxes(piece, 0, 1).reshape(piece.shape[1], -1).astype(jnp.float32)


def gather_narrow(weight):
    return lax.all_gather(weight, NARROW, axis=0, tiled=True)


def sum_narrow(partial):
    return lax.psum_scatter(
        partial.astype(jnp.bfloat16), NARROW, scatter_dimension=0, tiled=True
    ).astype(jnp.float32)


def rotate_heads(values, cosine, sine_table):
    half_size = HEAD_DIM // 2
    front_half = values[..., :half_size]
    back_half = values[..., half_size:]
    return jnp.concatenate(
        [
            front_half * cosine - back_half * sine_table,
            back_half * cosine + front_half * sine_table,
        ],
        axis=-1,
    )


def split_plan(
    wide,
    narrow,
    tokens,
    lengths,
    cotangent,
    norm1_gain,
    query_weight,
    key_weight,
    value_weight,
    out_weight,
    norm2_gain,
    gate_weight,
    up_weight,
    down_weight,
):
    micro_count, length, width = tokens.shape
    rows = micro_count * length
    sequences = wide * micro_count
    heads = width // HEAD_DIM // wide
    head_width = heads * HEAD_DIM
    hidden_width = gate_weight.shape[1] // wide
    position = jnp.arange(length, dtype=jnp.int32)
    row_mask = (position[None, :] < lengths).astype(jnp.float32).reshape(rows, 1)

    share = norm1_gain.shape[0]
    gains = jnp.concatenate([norm1_gain, norm2_gain])[None]
    gains = lax.all_to_all(
        jnp.broadcast_to(gains, (wide * narrow, 2 * share)),
        AXES,
        split_axis=0,
        concat_axis=0,
        tiled=True,
    ).astype(jnp.float32)
    gains = (gains[:, :share].reshape(width), gains[:, share:].reshape(width))
    attend_columns = to_columns(by_column((query_weight, key_weight, value_weight), wide))

    floats = tokens.reshape(rows, width).astype(jnp.float32)
    inverse_one = lax.rsqrt(jnp.mean(floats * floats, axis=-1, keepdims=True) + epsilon)
    normed_one = floats * inverse_one
    upstream = cotangent.reshape(rows, width).astype(jnp.float32) * row_mask
    upstream_all = gather_rows(upstream.astype(jnp.bfloat16), wide)
    feed_block, tokens_all, gains = lax.optimization_barrier(
        (
            by_column((gate_weight, up_weight), wide),
            gather_rows(tokens.reshape(rows, width), wide),
            gains,
        )
    )
    floats_all = tokens_all.astype(jnp.float32)
    inverse_all = lax.rsqrt(jnp.mean(floats_all * floats_all, axis=-1, keepdims=True) + epsilon)
    first_all = (floats_all * inverse_all * gains[0]).astype(jnp.bfloat16)
    feed_columns = to_columns(feed_block)
    out_rows = gather_narrow(out_weight)
    down_rows = gather_narrow(down_weight)

    cosine, sine_table = rotation_tables(length)
    cosine, sine_table = cosine[None, :, None, :], sine_table[None, :, None, :]
    joint = mixed_dot(first_all, attend_columns)
    by_head = (sequences, length, heads, HEAD_DIM)
    queries = rotate_heads(joint[:, :head_width].reshape(by_head), cosine, sine_table).astype(
        jnp.bfloat16
    )
    keys_rot = rotate_heads(
        joint[:, head_width : 2 * head_width].reshape(by_head), cosine, sine_table
    ).astype(jnp.bfloat16)
    values_all = joint[:, 2 * head_width :].reshape(by_head).astype(jnp.bfloat16)
    scores = jnp.einsum(
        "sqhd,skhd->shqk", queries, keys_rot, preferred_element_type=jnp.float32
    ) * HEAD_DIM ** (-0.5) - math.log(length)
    causal = (position[:, None] >= position[None, :]).astype(jnp.float32)
    gates_sig = jax.nn.sigmoid(scores)
    weights_low = (gates_sig * causal).astype(jnp.bfloat16)
    attended = (
        jnp.einsum("shqk,skhd->sqhd", weights_low, values_all, preferred_element_type=jnp.float32)
        .astype(jnp.bfloat16)
        .reshape(sequences * length, head_width)
    )
    out_term = mixed_dot(attended, out_rows).astype(jnp.bfloat16)
    middle = floats + scatter_rows(out_term, wide)

    inverse_two = lax.rsqrt(jnp.mean(middle * middle, axis=-1, keepdims=True) + epsilon)
    normed_two = middle * inverse_two
    second_all = gather_rows((normed_two * gains[1]).astype(jnp.bfloat16), wide)

    front = mixed_dot(second_all, feed_columns)
    gate_value = front[:, :hidden_width]
    up_value = front[:, hidden_width:]
    gate_sig = jax.nn.sigmoid(gate_value)
    hidden = (gate_value * gate_sig * up_value).astype(jnp.bfloat16)

    grad_hidden = back_dot(upstream_all, down_rows)
    grad_gate = (
        grad_hidden * up_value * gate_sig * (1.0 + gate_value * (1.0 - gate_sig))
    ).astype(jnp.bfloat16)
    grad_up = (grad_hidden * gate_value * gate_sig).astype(jnp.bfloat16)
    grad_front = jnp.concatenate([grad_gate, grad_up], axis=1)
    down_term, front_term, feed_term, second_term = lax.optimization_barrier(
        (
            outer_dot(hidden, upstream_all).astype(jnp.bfloat16),
            outer_dot(second_all, grad_front).astype(jnp.bfloat16),
            mixed_dot(hidden, down_rows).astype(jnp.bfloat16),
            back_dot(grad_front, feed_columns).astype(jnp.bfloat16),
        )
    )
    down_grad = sum_narrow(down_term)
    front_block = sum_blocks(front_term, wide)
    grad_second = scatter_rows(second_term, wide)
    feed_out = scatter_rows(feed_term, wide)
    front_block = to_rows(front_block)
    layer_output = ((middle + feed_out) * row_mask).astype(jnp.bfloat16)
    gate_grad = own_rows(front_block, 0, hidden_width)
    up_grad = own_rows(front_block, hidden_width, hidden_width)

    gain_two = jnp.sum(grad_second * normed_two, axis=0)
    grad_middle = upstream + norm_back(grad_second * gains[1], normed_two, inverse_two)
    middle_all = gather_rows(grad_middle.astype(jnp.bfloat16), wide)

    out_term, grad_attended = lax.optimization_barrier(
        (
            outer_dot(attended, middle_all).astype(jnp.bfloat16),
            back_dot(middle_all, out_rows).astype(jnp.bfloat16),
        )
    )
    grad_attended = grad_attended.reshape(by_head)
    out_grad = sum_narrow(out_term)
    grad_weights = jnp.einsum(
        "sqhd,skhd->shqk", grad_attended, values_all, preferred_element_type=jnp.float32
    )
    grad_values = jnp.einsum(
        "shqk,sqhd->skhd", weights_low, grad_attended, preferred_element_type=jnp.float32
    ).astype(jnp.bfloat16)
    grad_scores = (grad_weights * gates_sig * (1.0 - gates_sig) * causal).astype(jnp.bfloat16)
    scale_factor = HEAD_DIM ** (-0.5)
    query_rot = (
        jnp.einsum("shqk,skhd->sqhd", grad_scores, keys_rot, preferred_element_type=jnp.float32)
        * scale_factor
    )
    key_rot = (
        jnp.einsum("shqk,sqhd->skhd", grad_scores, queries, preferred_element_type=jnp.float32)
        * scale_factor
    )
    flat = (sequences * length, head_width)
    grad_joint = jnp.concatenate(
        [
            rotate_heads(query_rot, cosine, -sine_table).astype(jnp.bfloat16).reshape(flat),
            rotate_heads(key_rot, cosine, -sine_table).astype(jnp.bfloat16).reshape(flat),
            grad_values.reshape(flat),
        ],
        axis=1,
    )
    attend_term, first_term = lax.optimization_barrier(
        (
            outer_dot(first_all, grad_joint).astype(jnp.bfloat16),
            back_dot(grad_joint, attend_columns).astype(jnp.bfloat16),
        )
    )
    attend_block = sum_blocks(attend_term, wide)
    grad_first = scatter_rows(first_term, wide)
    attend_block = to_rows(attend_block)
    gain_one = jnp.sum(grad_first * normed_one, axis=0)
    input_grad = grad_middle + norm_back(grad_first * gains[0], normed_one, inverse_one)
    gain_terms = jnp.concatenate([gain_one.reshape(-1, share), gain_two.reshape(-1, share)], axis=1)
    gain_terms = lax.all_to_all(
        gain_terms, AXES, split_axis=0, concat_axis=0, tiled=True
    )
    gain_sums = jnp.sum(gain_terms, axis=0)
    return (
        layer_output.reshape(tokens.shape),
        input_grad.reshape(tokens.shape),
        gain_sums[:share],
        own_rows(attend_block, 0, head_width),
        own_rows(attend_block, head_width, head_width),
        own_rows(attend_block, 2 * head_width, head_width),
        out_grad,
        gain_sums[share:],
        gate_grad,
        up_grad,
        down_grad,
    )


def local(wide, narrow, *arrays):
    if arrays[0].shape[2] // HEAD_DIM % wide == 0:
        return split_plan(wide, narrow, *arrays)
    return gathered_plan(*arrays)


def solution(mesh):
    in_specs = (
        P(None, AXES, None),
        P(None, AXES),
        P(None, AXES, None),
        P(AXES),
        P(AXES, None),
        P(AXES, None),
        P(AXES, None),
        P(AXES, None),
        P(AXES),
        P(AXES, None),
        P(AXES, None),
        P(AXES, None),
    )
    out_specs = (
        P(None, AXES, None),
        P(None, AXES, None),
        P(AXES),
        P(AXES, None),
        P(AXES, None),
        P(AXES, None),
        P(AXES, None),
        P(AXES),
        P(AXES, None),
        P(AXES, None),
        P(AXES, None),
    )
    body = functools.partial(local, mesh.shape[WIDE], mesh.shape[NARROW])
    return jax.shard_map(body, mesh=mesh, in_specs=in_specs, out_specs=out_specs, check_vma=False)
```

```python
import functools
import math

import jax
import jax.numpy as jnp
from jax import lax
from jax.experimental import pallas as pl
from jax.experimental.pallas import tpu as pltpu
from jax.sharding import PartitionSpec as P


HEAD_DIM = 128
AXES = ("wide", "narrow")
WIDE, NARROW = AXES
MESH = pl.DeviceIdType.MESH
RING_COST = pl.CostEstimate(flops=0, bytes_accessed=150_000_000, transcendentals=0)


epsilon = 1e-05
rope_base = 10000.0


def mixed_dot(left, right):
    return jnp.dot(left, right, preferred_element_type=jnp.float32)


def outer_dot(left, right):
    return lax.dot_general(
        left, right, (((0,), (0,)), ((), ())), preferred_element_type=jnp.float32
    )


def back_dot(left, right):
    return lax.dot_general(
        left, right, (((1,), (1,)), ((), ())), preferred_element_type=jnp.float32
    )


def joined(pieces):
    return jnp.concatenate(pieces, axis=0)


def rotation_tables(length):
    half_size = HEAD_DIM // 2
    position = jnp.arange(length).astype(jnp.float32)
    frequency = rope_base ** (-jnp.arange(half_size).astype(jnp.float32) / half_size)
    angles = position[:, None] * frequency[None, :]
    return (jnp.cos(angles), jnp.sin(angles))


def rotate(values, cosine, sine_table):
    half_size = values.shape[-1] // 2
    front_half = values[..., :half_size]
    back_half = values[..., half_size:]
    cos_wide = cosine[:, None, :]
    sin_wide = sine_table[:, None, :]
    return jnp.concatenate(
        [
            front_half * cos_wide - back_half * sin_wide,
            back_half * cos_wide + front_half * sin_wide,
        ],
        axis=-1,
    )


def norm_back(grad_normed, normed, inverse):
    return inverse * (grad_normed - normed * jnp.mean(grad_normed * normed, axis=-1, keepdims=True))


def score_gates(queries, keys_rot):
    length = queries.shape[0]
    scores = jnp.einsum(
        "qhd,khd->hqk", queries, keys_rot, preferred_element_type=jnp.float32
    ) * HEAD_DIM ** (-0.5) - math.log(length)
    causal = (jnp.arange(length)[:, None] >= jnp.arange(length)[None, :]).astype(jnp.float32)
    return (jax.nn.sigmoid(scores), causal)


def attention_forward(inputs, attend_full):
    norm_gain, query_weight, key_weight, value_weight, out_weight = attend_full
    length, model_width = inputs.shape
    heads_count = model_width // HEAD_DIM
    floats = inputs.astype(jnp.float32)
    inverse = lax.rsqrt(jnp.mean(floats * floats, axis=-1, keepdims=True) + epsilon)
    normed = floats * inverse
    lowered = (normed * norm_gain.astype(jnp.float32)).astype(jnp.bfloat16)
    cosine, sine_table = rotation_tables(length)
    queries = rotate(
        mixed_dot(lowered, query_weight).reshape(length, heads_count, HEAD_DIM), cosine, sine_table
    ).astype(jnp.bfloat16)
    keys_rot = rotate(
        mixed_dot(lowered, key_weight).reshape(length, heads_count, HEAD_DIM), cosine, sine_table
    ).astype(jnp.bfloat16)
    values_all = (
        mixed_dot(lowered, value_weight).astype(jnp.bfloat16).reshape(length, heads_count, HEAD_DIM)
    )
    gates_sig, causal = score_gates(queries, keys_rot)
    weights_low = (gates_sig * causal).astype(jnp.bfloat16)
    attended = jnp.einsum(
        "hqk,khd->qhd", weights_low, values_all, preferred_element_type=jnp.float32
    )
    attended = attended.astype(jnp.bfloat16).reshape(length, model_width)
    middle = floats + mixed_dot(attended, out_weight)
    return (middle, (inverse, normed, lowered, queries, keys_rot, values_all, attended))


def feed_front(middle, front_full):
    norm_gain, gate_weight, up_weight = front_full
    inverse = lax.rsqrt(jnp.mean(middle * middle, axis=-1, keepdims=True) + epsilon)
    normed = middle * inverse
    lowered = (normed * norm_gain.astype(jnp.float32)).astype(jnp.bfloat16)
    gate_value = mixed_dot(lowered, gate_weight)
    up_value = mixed_dot(lowered, up_weight)
    hidden = (jax.nn.silu(gate_value) * up_value).astype(jnp.bfloat16)
    return (hidden, (inverse, normed, lowered, gate_value, up_value, hidden))


def attention_backward(grad_middle, saved_state, attend_full):
    norm_gain, query_weight, key_weight, value_weight, out_weight = attend_full
    inverse, normed, _, queries, keys_rot, values_all, _ = saved_state
    length, model_width = grad_middle.shape
    heads_count = model_width // HEAD_DIM
    grad_low = grad_middle.astype(jnp.bfloat16)
    grad_attended = (
        back_dot(grad_low, out_weight).astype(jnp.bfloat16).reshape(length, heads_count, HEAD_DIM)
    )
    gates_sig, causal = score_gates(queries, keys_rot)
    weights_low = (gates_sig * causal).astype(jnp.bfloat16)
    grad_weights = jnp.einsum(
        "qhd,khd->hqk", grad_attended, values_all, preferred_element_type=jnp.float32
    )
    grad_values = jnp.einsum(
        "hqk,qhd->khd", weights_low, grad_attended, preferred_element_type=jnp.float32
    )
    grad_values = grad_values.astype(jnp.bfloat16).reshape(length, model_width)
    grad_scores = (grad_weights * gates_sig * (1.0 - gates_sig) * causal).astype(jnp.bfloat16)
    scale_factor = HEAD_DIM ** (-0.5)
    cosine, sine_table = rotation_tables(length)
    query_rot = (
        jnp.einsum("hqk,khd->qhd", grad_scores, keys_rot, preferred_element_type=jnp.float32)
        * scale_factor
    )
    key_rot = (
        jnp.einsum("hqk,qhd->khd", grad_scores, queries, preferred_element_type=jnp.float32)
        * scale_factor
    )
    grad_queries = (
        rotate(query_rot, cosine, -sine_table).astype(jnp.bfloat16).reshape(length, model_width)
    )
    grad_keys = (
        rotate(key_rot, cosine, -sine_table).astype(jnp.bfloat16).reshape(length, model_width)
    )
    grad_lowered = (
        back_dot(grad_queries, query_weight)
        + back_dot(grad_keys, key_weight)
        + back_dot(grad_values, value_weight)
    )
    gain_term = jnp.sum(grad_lowered * normed, axis=0)
    grad_inputs = grad_middle + norm_back(
        grad_lowered * norm_gain.astype(jnp.float32), normed, inverse
    )
    return (grad_inputs, gain_term, (grad_queries, grad_keys, grad_values, grad_low))


def gathered_plan(
    tokens,
    lengths,
    cotangent,
    norm1_gain,
    query_weight,
    key_weight,
    value_weight,
    out_weight,
    norm2_gain,
    gate_weight,
    up_weight,
    down_weight,
):
    micro_count = tokens.shape[0]
    length = tokens.shape[1]
    position = jnp.arange(length, dtype=jnp.int32)
    row_masks = [
        (position < lengths[micro_index, 0]).astype(jnp.float32)
        for micro_index in range(micro_count)
    ]
    attend_full = (
        lax.all_gather(norm1_gain, AXES, axis=0, tiled=True),
        lax.all_gather(query_weight, AXES, axis=0, tiled=True),
        lax.all_gather(key_weight, AXES, axis=0, tiled=True),
        lax.all_gather(value_weight, AXES, axis=0, tiled=True),
        lax.all_gather(out_weight, AXES, axis=0, tiled=True),
    )
    middles = []
    attend_states = []
    for micro_index in range(micro_count):
        middle, attend_state = attention_forward(tokens[micro_index], attend_full)
        middles.append(middle)
        attend_states.append(attend_state)
    front_full = (
        lax.all_gather(norm2_gain, AXES, axis=0, tiled=True),
        lax.all_gather(gate_weight, AXES, axis=0, tiled=True),
        lax.all_gather(up_weight, AXES, axis=0, tiled=True),
    )
    feed_states = []
    for micro_index in range(micro_count):
        hidden, feed_state = feed_front(middles[micro_index], front_full)
        feed_states.append(feed_state)
    down_full = lax.all_gather(down_weight, AXES, axis=0, tiled=True)
    layer_rows = []
    for micro_index in range(micro_count):
        result = (
            middles[micro_index] + mixed_dot(feed_states[micro_index][5], down_full)
        ) * row_masks[micro_index][:, None]
        layer_rows.append(result.astype(jnp.bfloat16))
    down_back = lax.all_gather(down_weight, AXES, axis=0, tiled=True)
    upstreams = []
    upstream_lows = []
    grad_gates = []
    grad_ups = []
    for micro_index in range(micro_count):
        inverse, normed, lowered, gate_value, up_value, hidden = feed_states[micro_index]
        upstream = cotangent[micro_index].astype(jnp.float32) * row_masks[micro_index][:, None]
        upstream_low = upstream.astype(jnp.bfloat16)
        grad_hidden = back_dot(upstream_low, down_back)
        gate_sig = jax.nn.sigmoid(gate_value)
        grad_gates.append(
            (grad_hidden * up_value * gate_sig * (1.0 + gate_value * (1.0 - gate_sig))).astype(
                jnp.bfloat16
            )
        )
        grad_ups.append((grad_hidden * gate_value * gate_sig).astype(jnp.bfloat16))
        upstreams.append(upstream)
        upstream_lows.append(upstream_low)
    hidden_rows = joined([state[5] for state in feed_states])
    lowered_rows = joined([state[2] for state in feed_states])
    down_sum = lax.psum_scatter(
        outer_dot(hidden_rows, joined(upstream_lows)),
        AXES,
        scatter_dimension=0,
        tiled=True,
    )
    gain_two, gate_back = (
        lax.all_gather(norm2_gain, AXES, axis=0, tiled=True),
        lax.all_gather(gate_weight, AXES, axis=0, tiled=True),
    )
    grad_loweds = [
        back_dot(grad_gates[micro_index], gate_back) for micro_index in range(micro_count)
    ]
    gate_sum = lax.psum_scatter(
        outer_dot(lowered_rows, joined(grad_gates)),
        AXES,
        scatter_dimension=0,
        tiled=True,
    )
    up_back = lax.all_gather(up_weight, AXES, axis=0, tiled=True)
    gain_total = jnp.zeros((tokens.shape[2],), jnp.float32)
    grad_middles = []
    for micro_index in range(micro_count):
        inverse, normed, lowered, gate_value, up_value, hidden = feed_states[micro_index]
        grad_lowered = grad_loweds[micro_index] + back_dot(grad_ups[micro_index], up_back)
        gain_total = gain_total + jnp.sum(grad_lowered * normed, axis=0)
        grad_middles.append(
            upstreams[micro_index]
            + norm_back(grad_lowered * gain_two.astype(jnp.float32), normed, inverse)
        )
    up_total = outer_dot(lowered_rows, joined(grad_ups))
    gain_two_sum, up_sum = (
        lax.psum_scatter(gain_total, AXES, scatter_dimension=0, tiled=True),
        lax.psum_scatter(up_total, AXES, scatter_dimension=0, tiled=True),
    )
    attend_back = (
        lax.all_gather(norm1_gain, AXES, axis=0, tiled=True),
        lax.all_gather(query_weight, AXES, axis=0, tiled=True),
        lax.all_gather(key_weight, AXES, axis=0, tiled=True),
        lax.all_gather(value_weight, AXES, axis=0, tiled=True),
        lax.all_gather(out_weight, AXES, axis=0, tiled=True),
    )
    input_rows = []
    gain_first = jnp.zeros((tokens.shape[2],), jnp.float32)
    grad_lists = ([], [], [], [])
    for micro_index in range(micro_count):
        grad_inputs, gain_term, row_grads = attention_backward(
            grad_middles[micro_index], attend_states[micro_index], attend_back
        )
        input_rows.append(grad_inputs)
        gain_first = gain_first + gain_term
        for slot_index in range(4):
            grad_lists[slot_index].append(row_grads[slot_index])
    first_rows = joined([state[2] for state in attend_states])
    attended_rows = joined([state[6] for state in attend_states])
    query_total = outer_dot(first_rows, joined(grad_lists[0]))
    key_total = outer_dot(first_rows, joined(grad_lists[1]))
    value_total = outer_dot(first_rows, joined(grad_lists[2]))
    out_total = outer_dot(attended_rows, joined(grad_lists[3]))
    attend_sums = (
        lax.psum_scatter(gain_first, AXES, scatter_dimension=0, tiled=True),
        lax.psum_scatter(query_total, AXES, scatter_dimension=0, tiled=True),
        lax.psum_scatter(key_total, AXES, scatter_dimension=0, tiled=True),
        lax.psum_scatter(value_total, AXES, scatter_dimension=0, tiled=True),
        lax.psum_scatter(out_total, AXES, scatter_dimension=0, tiled=True),
    )
    layer_output = jnp.stack(layer_rows)
    input_grad = jnp.stack(input_rows)
    return (
        layer_output,
        input_grad,
        attend_sums[0],
        attend_sums[1],
        attend_sums[2],
        attend_sums[3],
        attend_sums[4],
        gain_two_sum,
        gate_sum,
        up_sum,
        down_sum,
    )


def ring_place(device, size):
    height, side = device // 2, device % 2
    return height * (1 - side) + (size - 1 - height) * side


def ring_device(place, size):
    back = place // (size // 2)
    return (1 - back) * 2 * place + back * (2 * (size - 1 - place) + 1)


def enter_ring(left, right):
    barrier = pltpu.get_barrier_semaphore()
    for device in (left, right):
        pl.semaphore_signal(barrier, inc=1, device_id={WIDE: device}, device_id_type=MESH)
    pl.semaphore_wait(barrier, 2)


def gather_kernel(size, block_ref, full_ref, own_sem, send_sem, recv_sem):
    place = ring_place(lax.axis_index(WIDE), size)
    left = ring_device((place + size - 1) % size, size)
    right = ring_device((place + 1) % size, size)
    half = block_ref.shape[0] // 2
    hops = size // 2

    def copy(way, hop, part):
        origin = ring_device((place + size - hop if way == 0 else place + hop) % size, size)
        target = full_ref.at[origin, pl.ds(part * half, half)]
        source = block_ref.at[pl.ds(part * half, half)] if hop == 0 else target
        return pltpu.make_async_remote_copy(
            src_ref=source,
            dst_ref=target,
            send_sem=send_sem.at[way, hop, part],
            recv_sem=recv_sem.at[way, hop, part],
            device_id={WIDE: right if way == 0 else left},
            device_id_type=MESH,
        )

    enter_ring(left, right)
    own = pltpu.make_async_copy(block_ref, full_ref.at[lax.axis_index(WIDE)], own_sem)
    sent = {}
    for hop in range(hops):
        for part in range(2):
            for way in range(2):
                if hop == hops - 1 and part != way:
                    continue
                if hop:
                    sent[way, hop - 1, part].wait_recv()
                sent[way, hop, part] = copy(way, hop, part)
                sent[way, hop, part].start()
        if hop == 0:
            own.start()
    for way in range(2):
        sent[way, hops - 2, 1 - way].wait_recv()
        sent[way, hops - 1, way].wait_recv()
    for transfer in sent.values():
        transfer.wait_send()
    own.wait()


def gather_rows(block, size):
    rows, width = block.shape
    hops = size // 2
    full = pl.pallas_call(
        functools.partial(gather_kernel, size),
        out_shape=jax.ShapeDtypeStruct((size, rows, width), block.dtype),
        in_specs=[pl.BlockSpec(memory_space=pltpu.VMEM)],
        out_specs=pl.BlockSpec(memory_space=pl.ANY),
        scratch_shapes=[
            pltpu.SemaphoreType.DMA,
            pltpu.SemaphoreType.DMA((2, hops, 2)),
            pltpu.SemaphoreType.DMA((2, hops, 2)),
        ],
        compiler_params=pltpu.CompilerParams(collective_id=0, has_side_effects=True),
        cost_estimate=RING_COST,
        name="gather_rows",
    )(block)
    return full.reshape(size * rows, width)


def feed_kernel(
    size,
    block_ref,
    second_ref,
    feed_ref,
    down_ref,
    full_ref,
    front_ref,
    hidden_ref,
    whole_ref,
    landed,
    feed,
    down,
    load_sem,
    keep_sem,
    store_sem,
    send_sem,
    recv_sem,
):
    me = lax.axis_index(WIDE)
    place = ring_place(me, size)
    left = ring_device((place + size - 1) % size, size)
    right = ring_device((place + 1) % size, size)
    half = block_ref.shape[0] // 2
    hops = size // 2
    tile = front_ref.shape[1] // (2 * hops)
    tall = second_ref.shape[0] // 2

    def origin(way, hop):
        return ring_device((place + size - hop if way == 0 else place + hop) % size, size)

    def copy(way, hop, part):
        target = landed.at[origin(way, hop), pl.ds(part * half, half)]
        return pltpu.make_async_remote_copy(
            src_ref=block_ref.at[pl.ds(part * half, half)] if hop == 0 else target,
            dst_ref=target,
            send_sem=send_sem.at[way, hop, part],
            recv_sem=recv_sem.at[way, hop, part],
            device_id={WIDE: right if way == 0 else left},
            device_id_type=MESH,
        )

    loads = [
        pltpu.make_async_copy(feed_ref.at[share], feed.at[:, share], load_sem.at[share])
        for share in range(feed_ref.shape[0])
    ]
    loads.append(pltpu.make_async_copy(down_ref, down, load_sem.at[feed_ref.shape[0]]))
    for load in loads:
        load.start()
    enter_ring(left, right)
    stores = []

    def front_tile(index):
        columns = pl.ds(index * tile, tile)
        weight = feed[:, :, :, columns].reshape(second_ref.shape[1], tile)

        def step(part, carry):
            rows = pl.ds(pl.multiple_of(part * tall, tall), tall)
            front_ref[rows, columns] = mixed_dot(second_ref[rows, :], weight)
            return carry

        lax.fori_loop(0, 2, step, 0)

    def use(source, owner, slot):
        store = pltpu.make_async_copy(source, full_ref.at[owner], store_sem.at[slot])
        store.start()
        stores.append(store)
        hidden_ref[owner] = back_dot(source[...], down[...])

    sent = {}
    for hop in range(hops):
        for part in range(2):
            for way in range(2):
                if hop == hops - 1 and part != way:
                    continue
                if hop:
                    sent[way, hop - 1, part].wait_recv()
                sent[way, hop, part] = copy(way, hop, part)
                sent[way, hop, part].start()
            if hop == 0 and part == 0:
                for load in loads:
                    load.wait()
                keep = pltpu.make_async_copy(feed, whole_ref, keep_sem)
                keep.start()
            front_tile(2 * hop + part)
        if hop == 0:
            use(block_ref, me, 0)
        for way in range(2):
            if hop == hops - 1:
                sent[way, hop - 1, 1 - way].wait_recv()
            if hop:
                use(landed.at[origin(way, hop)], origin(way, hop), 2 * hop - 1 + way)
    for way in range(2):
        sent[way, hops - 1, way].wait_recv()
    use(landed.at[origin(0, hops)], origin(0, hops), size - 1)
    for transfer in sent.values():
        transfer.wait_send()
    for store in stores:
        store.wait()
    keep.wait()


def gather_and_feed(block, second_all, feed_shares, down_rows, size):
    rows, width = block.shape
    narrow, _, share, columns = feed_shares.shape
    hidden = down_rows.shape[0]
    hops = size // 2
    full, front, grad_hidden, feed = pl.pallas_call(
        functools.partial(feed_kernel, size),
        out_shape=(
            jax.ShapeDtypeStruct((size, rows, width), block.dtype),
            jax.ShapeDtypeStruct((size * rows, columns), jnp.float32),
            jax.ShapeDtypeStruct((size, rows, hidden), jnp.float32),
            jax.ShapeDtypeStruct((size, narrow, share, columns), block.dtype),
        ),
        in_specs=[
            pl.BlockSpec(memory_space=pltpu.VMEM),
            pl.BlockSpec(memory_space=pltpu.VMEM),
            pl.BlockSpec(memory_space=pl.ANY),
            pl.BlockSpec(memory_space=pl.ANY),
        ],
        out_specs=(
            pl.BlockSpec(memory_space=pl.ANY),
            pl.BlockSpec(memory_space=pltpu.VMEM),
            pl.BlockSpec(memory_space=pltpu.VMEM),
            pl.BlockSpec(memory_space=pl.ANY),
        ),
        scratch_shapes=[
            pltpu.VMEM((size, rows, width), block.dtype),
            pltpu.VMEM((size, narrow, share, columns), block.dtype),
            pltpu.VMEM((hidden, width), block.dtype),
            pltpu.SemaphoreType.DMA((narrow + 1,)),
            pltpu.SemaphoreType.DMA,
            pltpu.SemaphoreType.DMA((size,)),
            pltpu.SemaphoreType.DMA((2, hops, 2)),
            pltpu.SemaphoreType.DMA((2, hops, 2)),
        ],
        compiler_params=pltpu.CompilerParams(collective_id=2, has_side_effects=True),
        cost_estimate=RING_COST,
    )(block, second_all, feed_shares, down_rows)
    return (
        full.reshape(size * rows, width),
        front,
        grad_hidden.reshape(size * rows, hidden),
        feed.reshape(-1, columns),
    )


def scatter_kernel(size, partial_ref, sum_ref, held, send_sem, recv_sem):
    place = ring_place(lax.axis_index(WIDE), size)
    left = ring_device((place + size - 1) % size, size)
    right = ring_device((place + 1) % size, size)
    rows, width = sum_ref.shape
    rows, width = rows // 2, width // 2

    def cut(way, part):
        return pl.ds(part * rows, rows), pl.ds(way * width, width)

    def mine(way, hop, part):
        block = ring_device((place + 2 * size - 1 - hop if way == 0 else place + 1 + hop) % size, size)
        return partial_ref.at[(block, *cut(way, part))]

    def copy(way, hop, part):
        source = mine(way, hop, part) if hop == 0 else held.at[(hop - 1, *cut(way, part))]
        return pltpu.make_async_remote_copy(
            src_ref=source,
            dst_ref=held.at[(hop, *cut(way, part))],
            send_sem=send_sem.at[way, hop, part],
            recv_sem=recv_sem.at[way, hop, part],
            device_id={WIDE: right if way == 0 else left},
            device_id_type=MESH,
        )

    enter_ring(left, right)
    sent = {}
    for hop in range(size):
        for part in range(2):
            for way in range(2):
                if hop:
                    sent[way, hop - 1, part].wait_recv()
                    arrived = held.at[(hop - 1, *cut(way, part))]
                    total = arrived[...].astype(jnp.float32) + mine(way, hop, part)[...].astype(
                        jnp.float32
                    )
                    if hop == size - 1:
                        sum_ref[cut(way, part)] = total
                        continue
                    arrived[...] = total.astype(jnp.bfloat16)
                sent[way, hop, part] = copy(way, hop, part)
                sent[way, hop, part].start()
    for transfer in sent.values():
        transfer.wait_send()


def scatter_rows(partial, size):
    rows, width = partial.shape[0] // size, partial.shape[1]
    steps = size - 1
    return pl.pallas_call(
        functools.partial(scatter_kernel, size),
        out_shape=jax.ShapeDtypeStruct((rows, width), jnp.float32),
        in_specs=[pl.BlockSpec(memory_space=pltpu.VMEM)],
        out_specs=pl.BlockSpec(memory_space=pltpu.VMEM),
        scratch_shapes=[
            pltpu.VMEM((steps, rows, width), jnp.bfloat16),
            pltpu.SemaphoreType.DMA((2, steps, 2)),
            pltpu.SemaphoreType.DMA((2, steps, 2)),
        ],
        compiler_params=pltpu.CompilerParams(collective_id=1, has_side_effects=True),
        cost_estimate=RING_COST,
        name="scatter_rows",
    )(partial.astype(jnp.bfloat16).reshape(size, rows, width))


def by_column(weights, wide):
    pieces = [w.reshape(w.shape[0], wide, w.shape[1] // wide) for w in weights]
    return jnp.swapaxes(jnp.concatenate(pieces, axis=2), 0, 1)


def to_columns(block):
    block = lax.all_to_all(block, WIDE, split_axis=0, concat_axis=0, tiled=True)
    full = lax.all_gather(block, NARROW, axis=1, tiled=True)
    return full.reshape(-1, full.shape[2])


def sum_blocks(columns, wide):
    rows, width = columns.shape
    block = columns.astype(jnp.bfloat16).reshape(wide, rows // wide, width)
    return lax.psum_scatter(block, NARROW, scatter_dimension=1, tiled=True)


def to_rows(block):
    return lax.all_to_all(block, WIDE, split_axis=0, concat_axis=0, tiled=True)


def own_rows(block, start, width):
    piece = block[:, :, start : start + width]
    return jnp.swapaxes(piece, 0, 1).reshape(piece.shape[1], -1).astype(jnp.float32)


def gather_narrow(weight):
    return lax.all_gather(weight, NARROW, axis=0, tiled=True)


def sum_narrow(partial):
    return lax.psum_scatter(
        partial.astype(jnp.bfloat16), NARROW, scatter_dimension=0, tiled=True
    ).astype(jnp.float32)


def rotate_heads(values, cosine, sine_table):
    half_size = HEAD_DIM // 2
    front_half = values[..., :half_size]
    back_half = values[..., half_size:]
    return jnp.concatenate(
        [
            front_half * cosine - back_half * sine_table,
            back_half * cosine + front_half * sine_table,
        ],
        axis=-1,
    )


def split_plan(
    wide,
    narrow,
    tokens,
    lengths,
    cotangent,
    norm1_gain,
    query_weight,
    key_weight,
    value_weight,
    out_weight,
    norm2_gain,
    gate_weight,
    up_weight,
    down_weight,
):
    micro_count, length, width = tokens.shape
    rows = micro_count * length
    sequences = wide * micro_count
    heads = width // HEAD_DIM // wide
    head_width = heads * HEAD_DIM
    hidden_width = gate_weight.shape[1] // wide
    position = jnp.arange(length, dtype=jnp.int32)
    row_mask = (position[None, :] < lengths).astype(jnp.float32).reshape(rows, 1)

    share = norm1_gain.shape[0]
    gains = jnp.concatenate([norm1_gain, norm2_gain])[None]
    gains = lax.all_to_all(
        jnp.broadcast_to(gains, (wide * narrow, 2 * share)),
        AXES,
        split_axis=0,
        concat_axis=0,
        tiled=True,
    ).astype(jnp.float32)
    gains = (gains[:, :share].reshape(width), gains[:, share:].reshape(width))
    attend_columns = to_columns(by_column((query_weight, key_weight, value_weight), wide))

    floats = tokens.reshape(rows, width).astype(jnp.float32)
    inverse_one = lax.rsqrt(jnp.mean(floats * floats, axis=-1, keepdims=True) + epsilon)
    normed_one = floats * inverse_one
    upstream = cotangent.reshape(rows, width).astype(jnp.float32) * row_mask
    feed_block, tokens_all, gains = lax.optimization_barrier(
        (
            by_column((gate_weight, up_weight), wide),
            gather_rows(tokens.reshape(rows, width), wide),
            gains,
        )
    )
    floats_all = tokens_all.astype(jnp.float32)
    inverse_all = lax.rsqrt(jnp.mean(floats_all * floats_all, axis=-1, keepdims=True) + epsilon)
    first_all = (floats_all * inverse_all * gains[0]).astype(jnp.bfloat16)
    feed_block = lax.all_to_all(feed_block, WIDE, split_axis=0, concat_axis=0, tiled=True)
    feed_shares = lax.all_gather(feed_block, NARROW)
    out_rows = gather_narrow(out_weight)
    down_rows = gather_narrow(down_weight)

    cosine, sine_table = rotation_tables(length)
    cosine, sine_table = cosine[None, :, None, :], sine_table[None, :, None, :]
    joint = mixed_dot(first_all, attend_columns)
    by_head = (sequences, length, heads, HEAD_DIM)
    queries = rotate_heads(joint[:, :head_width].reshape(by_head), cosine, sine_table).astype(
        jnp.bfloat16
    )
    keys_rot = rotate_heads(
        joint[:, head_width : 2 * head_width].reshape(by_head), cosine, sine_table
    ).astype(jnp.bfloat16)
    values_all = joint[:, 2 * head_width :].reshape(by_head).astype(jnp.bfloat16)
    scores = jnp.einsum(
        "sqhd,skhd->shqk", queries, keys_rot, preferred_element_type=jnp.float32
    ) * HEAD_DIM ** (-0.5) - math.log(length)
    causal = (position[:, None] >= position[None, :]).astype(jnp.float32)
    gates_sig = jax.nn.sigmoid(scores)
    weights_low = (gates_sig * causal).astype(jnp.bfloat16)
    attended = (
        jnp.einsum("shqk,skhd->sqhd", weights_low, values_all, preferred_element_type=jnp.float32)
        .astype(jnp.bfloat16)
        .reshape(sequences * length, head_width)
    )
    out_term = mixed_dot(attended, out_rows).astype(jnp.bfloat16)
    middle = floats + scatter_rows(out_term, wide)

    inverse_two = lax.rsqrt(jnp.mean(middle * middle, axis=-1, keepdims=True) + epsilon)
    normed_two = middle * inverse_two
    second_all = gather_rows((normed_two * gains[1]).astype(jnp.bfloat16), wide)

    upstream_all, front, grad_hidden, feed_columns = gather_and_feed(
        upstream.astype(jnp.bfloat16), second_all, feed_shares, down_rows, wide
    )
    gate_value = front[:, :hidden_width]
    up_value = front[:, hidden_width:]
    gate_sig = jax.nn.sigmoid(gate_value)
    hidden = (gate_value * gate_sig * up_value).astype(jnp.bfloat16)

    grad_gate = (
        grad_hidden * up_value * gate_sig * (1.0 + gate_value * (1.0 - gate_sig))
    ).astype(jnp.bfloat16)
    grad_up = (grad_hidden * gate_value * gate_sig).astype(jnp.bfloat16)
    grad_front = jnp.concatenate([grad_gate, grad_up], axis=1)
    down_term, front_term, feed_term, second_term = lax.optimization_barrier(
        (
            outer_dot(hidden, upstream_all).astype(jnp.bfloat16),
            outer_dot(second_all, grad_front).astype(jnp.bfloat16),
            mixed_dot(hidden, down_rows).astype(jnp.bfloat16),
            back_dot(grad_front, feed_columns).astype(jnp.bfloat16),
        )
    )
    down_grad = sum_narrow(down_term)
    front_block = sum_blocks(front_term, wide)
    grad_second = scatter_rows(second_term, wide)
    feed_out = scatter_rows(feed_term, wide)
    front_block = to_rows(front_block)
    layer_output = ((middle + feed_out) * row_mask).astype(jnp.bfloat16)
    gate_grad = own_rows(front_block, 0, hidden_width)
    up_grad = own_rows(front_block, hidden_width, hidden_width)

    gain_two = jnp.sum(grad_second * normed_two, axis=0)
    grad_middle = upstream + norm_back(grad_second * gains[1], normed_two, inverse_two)
    middle_all = gather_rows(grad_middle.astype(jnp.bfloat16), wide)

    out_term, grad_attended = lax.optimization_barrier(
        (
            outer_dot(attended, middle_all).astype(jnp.bfloat16),
            back_dot(middle_all, out_rows).astype(jnp.bfloat16),
        )
    )
    grad_attended = grad_attended.reshape(by_head)
    out_grad = sum_narrow(out_term)
    grad_weights = jnp.einsum(
        "sqhd,skhd->shqk", grad_attended, values_all, preferred_element_type=jnp.float32
    )
    grad_values = jnp.einsum(
        "shqk,sqhd->skhd", weights_low, grad_attended, preferred_element_type=jnp.float32
    ).astype(jnp.bfloat16)
    grad_scores = (grad_weights * gates_sig * (1.0 - gates_sig) * causal).astype(jnp.bfloat16)
    scale_factor = HEAD_DIM ** (-0.5)
    query_rot = (
        jnp.einsum("shqk,skhd->sqhd", grad_scores, keys_rot, preferred_element_type=jnp.float32)
        * scale_factor
    )
    key_rot = (
        jnp.einsum("shqk,sqhd->skhd", grad_scores, queries, preferred_element_type=jnp.float32)
        * scale_factor
    )
    flat = (sequences * length, head_width)
    grad_joint = jnp.concatenate(
        [
            rotate_heads(query_rot, cosine, -sine_table).astype(jnp.bfloat16).reshape(flat),
            rotate_heads(key_rot, cosine, -sine_table).astype(jnp.bfloat16).reshape(flat),
            grad_values.reshape(flat),
        ],
        axis=1,
    )
    attend_term, first_term = lax.optimization_barrier(
        (
            outer_dot(first_all, grad_joint).astype(jnp.bfloat16),
            back_dot(grad_joint, attend_columns).astype(jnp.bfloat16),
        )
    )
    attend_block = sum_blocks(attend_term, wide)
    grad_first = scatter_rows(first_term, wide)
    attend_block = to_rows(attend_block)
    gain_one = jnp.sum(grad_first * normed_one, axis=0)
    input_grad = grad_middle + norm_back(grad_first * gains[0], normed_one, inverse_one)
    gain_terms = jnp.concatenate([gain_one.reshape(-1, share), gain_two.reshape(-1, share)], axis=1)
    gain_terms = lax.all_to_all(
        gain_terms, AXES, split_axis=0, concat_axis=0, tiled=True
    )
    gain_sums = jnp.sum(gain_terms, axis=0)
    return (
        layer_output.reshape(tokens.shape),
        input_grad.reshape(tokens.shape),
        gain_sums[:share],
        own_rows(attend_block, 0, head_width),
        own_rows(attend_block, head_width, head_width),
        own_rows(attend_block, 2 * head_width, head_width),
        out_grad,
        gain_sums[share:],
        gate_grad,
        up_grad,
        down_grad,
    )


def local(wide, narrow, *arrays):
    if arrays[0].shape[2] // HEAD_DIM % wide == 0:
        return split_plan(wide, narrow, *arrays)
    return gathered_plan(*arrays)


def solution(mesh):
    in_specs = (
        P(None, AXES, None),
        P(None, AXES),
        P(None, AXES, None),
        P(AXES),
        P(AXES, None),
        P(AXES, None),
        P(AXES, None),
        P(AXES, None),
        P(AXES),
        P(AXES, None),
        P(AXES, None),
        P(AXES, None),
    )
    out_specs = (
        P(None, AXES, None),
        P(None, AXES, None),
        P(AXES),
        P(AXES, None),
        P(AXES, None),
        P(AXES, None),
        P(AXES, None),
        P(AXES),
        P(AXES, None),
        P(AXES, None),
        P(AXES, None),
    )
    body = functools.partial(local, mesh.shape[WIDE], mesh.shape[NARROW])
    return jax.shard_map(body, mesh=mesh, in_specs=in_specs, out_specs=out_specs, check_vma=False)
```

```python
import functools
import math

import jax
import jax.numpy as jnp
from jax import lax
from jax.experimental import pallas as pl
from jax.experimental.pallas import tpu as pltpu
from jax.sharding import PartitionSpec as P


HEAD_DIM = 128
AXES = ("wide", "narrow")
WIDE, NARROW = AXES
MESH = pl.DeviceIdType.MESH
RING_COST = pl.CostEstimate(flops=0, bytes_accessed=150_000_000, transcendentals=0)


epsilon = 1e-05
rope_base = 10000.0


def mixed_dot(left, right):
    return jnp.dot(left, right, preferred_element_type=jnp.float32)


def outer_dot(left, right):
    return lax.dot_general(
        left, right, (((0,), (0,)), ((), ())), preferred_element_type=jnp.float32
    )


def back_dot(left, right):
    return lax.dot_general(
        left, right, (((1,), (1,)), ((), ())), preferred_element_type=jnp.float32
    )


def joined(pieces):
    return jnp.concatenate(pieces, axis=0)


def rotation_tables(length):
    half_size = HEAD_DIM // 2
    position = jnp.arange(length).astype(jnp.float32)
    frequency = rope_base ** (-jnp.arange(half_size).astype(jnp.float32) / half_size)
    angles = position[:, None] * frequency[None, :]
    return (jnp.cos(angles), jnp.sin(angles))


def rotate(values, cosine, sine_table):
    half_size = values.shape[-1] // 2
    front_half = values[..., :half_size]
    back_half = values[..., half_size:]
    cos_wide = cosine[:, None, :]
    sin_wide = sine_table[:, None, :]
    return jnp.concatenate(
        [
            front_half * cos_wide - back_half * sin_wide,
            back_half * cos_wide + front_half * sin_wide,
        ],
        axis=-1,
    )


def norm_back(grad_normed, normed, inverse):
    return inverse * (grad_normed - normed * jnp.mean(grad_normed * normed, axis=-1, keepdims=True))


def score_gates(queries, keys_rot):
    length = queries.shape[0]
    scores = jnp.einsum(
        "qhd,khd->hqk", queries, keys_rot, preferred_element_type=jnp.float32
    ) * HEAD_DIM ** (-0.5) - math.log(length)
    causal = (jnp.arange(length)[:, None] >= jnp.arange(length)[None, :]).astype(jnp.float32)
    return (jax.nn.sigmoid(scores), causal)


def attention_forward(inputs, attend_full):
    norm_gain, query_weight, key_weight, value_weight, out_weight = attend_full
    length, model_width = inputs.shape
    heads_count = model_width // HEAD_DIM
    floats = inputs.astype(jnp.float32)
    inverse = lax.rsqrt(jnp.mean(floats * floats, axis=-1, keepdims=True) + epsilon)
    normed = floats * inverse
    lowered = (normed * norm_gain.astype(jnp.float32)).astype(jnp.bfloat16)
    cosine, sine_table = rotation_tables(length)
    queries = rotate(
        mixed_dot(lowered, query_weight).reshape(length, heads_count, HEAD_DIM), cosine, sine_table
    ).astype(jnp.bfloat16)
    keys_rot = rotate(
        mixed_dot(lowered, key_weight).reshape(length, heads_count, HEAD_DIM), cosine, sine_table
    ).astype(jnp.bfloat16)
    values_all = (
        mixed_dot(lowered, value_weight).astype(jnp.bfloat16).reshape(length, heads_count, HEAD_DIM)
    )
    gates_sig, causal = score_gates(queries, keys_rot)
    weights_low = (gates_sig * causal).astype(jnp.bfloat16)
    attended = jnp.einsum(
        "hqk,khd->qhd", weights_low, values_all, preferred_element_type=jnp.float32
    )
    attended = attended.astype(jnp.bfloat16).reshape(length, model_width)
    middle = floats + mixed_dot(attended, out_weight)
    return (middle, (inverse, normed, lowered, queries, keys_rot, values_all, attended))


def feed_front(middle, front_full):
    norm_gain, gate_weight, up_weight = front_full
    inverse = lax.rsqrt(jnp.mean(middle * middle, axis=-1, keepdims=True) + epsilon)
    normed = middle * inverse
    lowered = (normed * norm_gain.astype(jnp.float32)).astype(jnp.bfloat16)
    gate_value = mixed_dot(lowered, gate_weight)
    up_value = mixed_dot(lowered, up_weight)
    hidden = (jax.nn.silu(gate_value) * up_value).astype(jnp.bfloat16)
    return (hidden, (inverse, normed, lowered, gate_value, up_value, hidden))


def attention_backward(grad_middle, saved_state, attend_full):
    norm_gain, query_weight, key_weight, value_weight, out_weight = attend_full
    inverse, normed, _, queries, keys_rot, values_all, _ = saved_state
    length, model_width = grad_middle.shape
    heads_count = model_width // HEAD_DIM
    grad_low = grad_middle.astype(jnp.bfloat16)
    grad_attended = (
        back_dot(grad_low, out_weight).astype(jnp.bfloat16).reshape(length, heads_count, HEAD_DIM)
    )
    gates_sig, causal = score_gates(queries, keys_rot)
    weights_low = (gates_sig * causal).astype(jnp.bfloat16)
    grad_weights = jnp.einsum(
        "qhd,khd->hqk", grad_attended, values_all, preferred_element_type=jnp.float32
    )
    grad_values = jnp.einsum(
        "hqk,qhd->khd", weights_low, grad_attended, preferred_element_type=jnp.float32
    )
    grad_values = grad_values.astype(jnp.bfloat16).reshape(length, model_width)
    grad_scores = (grad_weights * gates_sig * (1.0 - gates_sig) * causal).astype(jnp.bfloat16)
    scale_factor = HEAD_DIM ** (-0.5)
    cosine, sine_table = rotation_tables(length)
    query_rot = (
        jnp.einsum("hqk,khd->qhd", grad_scores, keys_rot, preferred_element_type=jnp.float32)
        * scale_factor
    )
    key_rot = (
        jnp.einsum("hqk,qhd->khd", grad_scores, queries, preferred_element_type=jnp.float32)
        * scale_factor
    )
    grad_queries = (
        rotate(query_rot, cosine, -sine_table).astype(jnp.bfloat16).reshape(length, model_width)
    )
    grad_keys = (
        rotate(key_rot, cosine, -sine_table).astype(jnp.bfloat16).reshape(length, model_width)
    )
    grad_lowered = (
        back_dot(grad_queries, query_weight)
        + back_dot(grad_keys, key_weight)
        + back_dot(grad_values, value_weight)
    )
    gain_term = jnp.sum(grad_lowered * normed, axis=0)
    grad_inputs = grad_middle + norm_back(
        grad_lowered * norm_gain.astype(jnp.float32), normed, inverse
    )
    return (grad_inputs, gain_term, (grad_queries, grad_keys, grad_values, grad_low))


def gathered_plan(
    tokens,
    lengths,
    cotangent,
    norm1_gain,
    query_weight,
    key_weight,
    value_weight,
    out_weight,
    norm2_gain,
    gate_weight,
    up_weight,
    down_weight,
):
    micro_count = tokens.shape[0]
    length = tokens.shape[1]
    position = jnp.arange(length, dtype=jnp.int32)
    row_masks = [
        (position < lengths[micro_index, 0]).astype(jnp.float32)
        for micro_index in range(micro_count)
    ]
    attend_full = (
        lax.all_gather(norm1_gain, AXES, axis=0, tiled=True),
        lax.all_gather(query_weight, AXES, axis=0, tiled=True),
        lax.all_gather(key_weight, AXES, axis=0, tiled=True),
        lax.all_gather(value_weight, AXES, axis=0, tiled=True),
        lax.all_gather(out_weight, AXES, axis=0, tiled=True),
    )
    middles = []
    attend_states = []
    for micro_index in range(micro_count):
        middle, attend_state = attention_forward(tokens[micro_index], attend_full)
        middles.append(middle)
        attend_states.append(attend_state)
    front_full = (
        lax.all_gather(norm2_gain, AXES, axis=0, tiled=True),
        lax.all_gather(gate_weight, AXES, axis=0, tiled=True),
        lax.all_gather(up_weight, AXES, axis=0, tiled=True),
    )
    feed_states = []
    for micro_index in range(micro_count):
        hidden, feed_state = feed_front(middles[micro_index], front_full)
        feed_states.append(feed_state)
    down_full = lax.all_gather(down_weight, AXES, axis=0, tiled=True)
    layer_rows = []
    for micro_index in range(micro_count):
        result = (
            middles[micro_index] + mixed_dot(feed_states[micro_index][5], down_full)
        ) * row_masks[micro_index][:, None]
        layer_rows.append(result.astype(jnp.bfloat16))
    down_back = lax.all_gather(down_weight, AXES, axis=0, tiled=True)
    upstreams = []
    upstream_lows = []
    grad_gates = []
    grad_ups = []
    for micro_index in range(micro_count):
        inverse, normed, lowered, gate_value, up_value, hidden = feed_states[micro_index]
        upstream = cotangent[micro_index].astype(jnp.float32) * row_masks[micro_index][:, None]
        upstream_low = upstream.astype(jnp.bfloat16)
        grad_hidden = back_dot(upstream_low, down_back)
        gate_sig = jax.nn.sigmoid(gate_value)
        grad_gates.append(
            (grad_hidden * up_value * gate_sig * (1.0 + gate_value * (1.0 - gate_sig))).astype(
                jnp.bfloat16
            )
        )
        grad_ups.append((grad_hidden * gate_value * gate_sig).astype(jnp.bfloat16))
        upstreams.append(upstream)
        upstream_lows.append(upstream_low)
    hidden_rows = joined([state[5] for state in feed_states])
    lowered_rows = joined([state[2] for state in feed_states])
    down_sum = lax.psum_scatter(
        outer_dot(hidden_rows, joined(upstream_lows)),
        AXES,
        scatter_dimension=0,
        tiled=True,
    )
    gain_two, gate_back = (
        lax.all_gather(norm2_gain, AXES, axis=0, tiled=True),
        lax.all_gather(gate_weight, AXES, axis=0, tiled=True),
    )
    grad_loweds = [
        back_dot(grad_gates[micro_index], gate_back) for micro_index in range(micro_count)
    ]
    gate_sum = lax.psum_scatter(
        outer_dot(lowered_rows, joined(grad_gates)),
        AXES,
        scatter_dimension=0,
        tiled=True,
    )
    up_back = lax.all_gather(up_weight, AXES, axis=0, tiled=True)
    gain_total = jnp.zeros((tokens.shape[2],), jnp.float32)
    grad_middles = []
    for micro_index in range(micro_count):
        inverse, normed, lowered, gate_value, up_value, hidden = feed_states[micro_index]
        grad_lowered = grad_loweds[micro_index] + back_dot(grad_ups[micro_index], up_back)
        gain_total = gain_total + jnp.sum(grad_lowered * normed, axis=0)
        grad_middles.append(
            upstreams[micro_index]
            + norm_back(grad_lowered * gain_two.astype(jnp.float32), normed, inverse)
        )
    up_total = outer_dot(lowered_rows, joined(grad_ups))
    gain_two_sum, up_sum = (
        lax.psum_scatter(gain_total, AXES, scatter_dimension=0, tiled=True),
        lax.psum_scatter(up_total, AXES, scatter_dimension=0, tiled=True),
    )
    attend_back = (
        lax.all_gather(norm1_gain, AXES, axis=0, tiled=True),
        lax.all_gather(query_weight, AXES, axis=0, tiled=True),
        lax.all_gather(key_weight, AXES, axis=0, tiled=True),
        lax.all_gather(value_weight, AXES, axis=0, tiled=True),
        lax.all_gather(out_weight, AXES, axis=0, tiled=True),
    )
    input_rows = []
    gain_first = jnp.zeros((tokens.shape[2],), jnp.float32)
    grad_lists = ([], [], [], [])
    for micro_index in range(micro_count):
        grad_inputs, gain_term, row_grads = attention_backward(
            grad_middles[micro_index], attend_states[micro_index], attend_back
        )
        input_rows.append(grad_inputs)
        gain_first = gain_first + gain_term
        for slot_index in range(4):
            grad_lists[slot_index].append(row_grads[slot_index])
    first_rows = joined([state[2] for state in attend_states])
    attended_rows = joined([state[6] for state in attend_states])
    query_total = outer_dot(first_rows, joined(grad_lists[0]))
    key_total = outer_dot(first_rows, joined(grad_lists[1]))
    value_total = outer_dot(first_rows, joined(grad_lists[2]))
    out_total = outer_dot(attended_rows, joined(grad_lists[3]))
    attend_sums = (
        lax.psum_scatter(gain_first, AXES, scatter_dimension=0, tiled=True),
        lax.psum_scatter(query_total, AXES, scatter_dimension=0, tiled=True),
        lax.psum_scatter(key_total, AXES, scatter_dimension=0, tiled=True),
        lax.psum_scatter(value_total, AXES, scatter_dimension=0, tiled=True),
        lax.psum_scatter(out_total, AXES, scatter_dimension=0, tiled=True),
    )
    layer_output = jnp.stack(layer_rows)
    input_grad = jnp.stack(input_rows)
    return (
        layer_output,
        input_grad,
        attend_sums[0],
        attend_sums[1],
        attend_sums[2],
        attend_sums[3],
        attend_sums[4],
        gain_two_sum,
        gate_sum,
        up_sum,
        down_sum,
    )


def ring_place(device, size):
    height, side = device // 2, device % 2
    return height * (1 - side) + (size - 1 - height) * side


def ring_device(place, size):
    back = place // (size // 2)
    return (1 - back) * 2 * place + back * (2 * (size - 1 - place) + 1)


def enter_ring(left, right):
    barrier = pltpu.get_barrier_semaphore()
    for device in (left, right):
        pl.semaphore_signal(barrier, inc=1, device_id={WIDE: device}, device_id_type=MESH)
    pl.semaphore_wait(barrier, 2)


def gather_kernel(size, block_ref, full_ref, own_sem, send_sem, recv_sem):
    place = ring_place(lax.axis_index(WIDE), size)
    left = ring_device((place + size - 1) % size, size)
    right = ring_device((place + 1) % size, size)
    half = block_ref.shape[0] // 2
    hops = size // 2

    def copy(way, hop, part):
        origin = ring_device((place + size - hop if way == 0 else place + hop) % size, size)
        target = full_ref.at[origin, pl.ds(part * half, half)]
        source = block_ref.at[pl.ds(part * half, half)] if hop == 0 else target
        return pltpu.make_async_remote_copy(
            src_ref=source,
            dst_ref=target,
            send_sem=send_sem.at[way, hop, part],
            recv_sem=recv_sem.at[way, hop, part],
            device_id={WIDE: right if way == 0 else left},
            device_id_type=MESH,
        )

    enter_ring(left, right)
    own = pltpu.make_async_copy(block_ref, full_ref.at[lax.axis_index(WIDE)], own_sem)
    sent = {}
    for hop in range(hops):
        for part in range(2):
            for way in range(2):
                if hop == hops - 1 and part != way:
                    continue
                if hop:
                    sent[way, hop - 1, part].wait_recv()
                sent[way, hop, part] = copy(way, hop, part)
                sent[way, hop, part].start()
        if hop == 0:
            own.start()
    for way in range(2):
        sent[way, hops - 2, 1 - way].wait_recv()
        sent[way, hops - 1, way].wait_recv()
    for transfer in sent.values():
        transfer.wait_send()
    own.wait()


def gather_rows(block, size):
    rows, width = block.shape
    hops = size // 2
    full = pl.pallas_call(
        functools.partial(gather_kernel, size),
        out_shape=jax.ShapeDtypeStruct((size, rows, width), block.dtype),
        in_specs=[pl.BlockSpec(memory_space=pltpu.VMEM)],
        out_specs=pl.BlockSpec(memory_space=pl.ANY),
        scratch_shapes=[
            pltpu.SemaphoreType.DMA,
            pltpu.SemaphoreType.DMA((2, hops, 2)),
            pltpu.SemaphoreType.DMA((2, hops, 2)),
        ],
        compiler_params=pltpu.CompilerParams(collective_id=0, has_side_effects=True),
        cost_estimate=RING_COST,
        name="gather_rows",
    )(block)
    return full.reshape(size * rows, width)


def feed_kernel(
    size,
    block_ref,
    second_ref,
    feed_ref,
    down_ref,
    full_ref,
    front_ref,
    hidden_ref,
    whole_ref,
    landed,
    feed,
    down,
    load_sem,
    keep_sem,
    store_sem,
    send_sem,
    recv_sem,
):
    me = lax.axis_index(WIDE)
    place = ring_place(me, size)
    left = ring_device((place + size - 1) % size, size)
    right = ring_device((place + 1) % size, size)
    half = block_ref.shape[0] // 2
    hops = size // 2
    tile = front_ref.shape[1] // (2 * hops)
    tall = second_ref.shape[0] // 2

    def origin(way, hop):
        return ring_device((place + size - hop if way == 0 else place + hop) % size, size)

    def copy(way, hop, part):
        target = landed.at[origin(way, hop), pl.ds(part * half, half)]
        return pltpu.make_async_remote_copy(
            src_ref=block_ref.at[pl.ds(part * half, half)] if hop == 0 else target,
            dst_ref=target,
            send_sem=send_sem.at[way, hop, part],
            recv_sem=recv_sem.at[way, hop, part],
            device_id={WIDE: right if way == 0 else left},
            device_id_type=MESH,
        )

    loads = [
        pltpu.make_async_copy(feed_ref.at[share], feed.at[:, share], load_sem.at[share])
        for share in range(feed_ref.shape[0])
    ]
    loads.append(pltpu.make_async_copy(down_ref, down, load_sem.at[feed_ref.shape[0]]))
    for load in loads:
        load.start()
    enter_ring(left, right)
    stores = []

    def front_tile(index):
        columns = pl.ds(index * tile, tile)
        weight = feed[:, :, :, columns].reshape(second_ref.shape[1], tile)

        def step(part, carry):
            rows = pl.ds(pl.multiple_of(part * tall, tall), tall)
            front_ref[rows, columns] = mixed_dot(second_ref[rows, :], weight)
            return carry

        lax.fori_loop(0, 2, step, 0)

    def use(source, owner, slot):
        store = pltpu.make_async_copy(source, full_ref.at[owner], store_sem.at[slot])
        store.start()
        stores.append(store)
        hidden_ref[owner] = back_dot(source[...], down[...])

    sent = {}
    for hop in range(hops):
        for part in range(2):
            for way in range(2):
                if hop == hops - 1 and part != way:
                    continue
                if hop:
                    sent[way, hop - 1, part].wait_recv()
                sent[way, hop, part] = copy(way, hop, part)
                sent[way, hop, part].start()
            if hop == 0 and part == 0:
                for load in loads:
                    load.wait()
                keep = pltpu.make_async_copy(feed, whole_ref, keep_sem)
                keep.start()
            front_tile(2 * hop + part)
        if hop == 0:
            use(block_ref, me, 0)
        for way in range(2):
            if hop == hops - 1:
                sent[way, hop - 1, 1 - way].wait_recv()
            if hop:
                use(landed.at[origin(way, hop)], origin(way, hop), 2 * hop - 1 + way)
    for way in range(2):
        sent[way, hops - 1, way].wait_recv()
    use(landed.at[origin(0, hops)], origin(0, hops), size - 1)
    for transfer in sent.values():
        transfer.wait_send()
    for store in stores:
        store.wait()
    keep.wait()


def gather_and_feed(block, second_all, feed_shares, down_rows, size):
    rows, width = block.shape
    narrow, _, share, columns = feed_shares.shape
    hidden = down_rows.shape[0]
    hops = size // 2
    full, front, grad_hidden, feed = pl.pallas_call(
        functools.partial(feed_kernel, size),
        out_shape=(
            jax.ShapeDtypeStruct((size, rows, width), block.dtype),
            jax.ShapeDtypeStruct((size * rows, columns), jnp.float32),
            jax.ShapeDtypeStruct((size, rows, hidden), jnp.float32),
            jax.ShapeDtypeStruct((size, narrow, share, columns), block.dtype),
        ),
        in_specs=[
            pl.BlockSpec(memory_space=pltpu.VMEM),
            pl.BlockSpec(memory_space=pltpu.VMEM),
            pl.BlockSpec(memory_space=pl.ANY),
            pl.BlockSpec(memory_space=pl.ANY),
        ],
        out_specs=(
            pl.BlockSpec(memory_space=pl.ANY),
            pl.BlockSpec(memory_space=pltpu.VMEM),
            pl.BlockSpec(memory_space=pltpu.VMEM),
            pl.BlockSpec(memory_space=pl.ANY),
        ),
        scratch_shapes=[
            pltpu.VMEM((size, rows, width), block.dtype),
            pltpu.VMEM((size, narrow, share, columns), block.dtype),
            pltpu.VMEM((hidden, width), block.dtype),
            pltpu.SemaphoreType.DMA((narrow + 1,)),
            pltpu.SemaphoreType.DMA,
            pltpu.SemaphoreType.DMA((size,)),
            pltpu.SemaphoreType.DMA((2, hops, 2)),
            pltpu.SemaphoreType.DMA((2, hops, 2)),
        ],
        compiler_params=pltpu.CompilerParams(collective_id=2, has_side_effects=True),
        cost_estimate=RING_COST,
    )(block, second_all, feed_shares, down_rows)
    return (
        full.reshape(size * rows, width),
        front,
        grad_hidden.reshape(size * rows, hidden),
        feed.reshape(-1, columns),
    )


def scatter_kernel(size, flipped, left_ref, right_ref, sum_ref, term, first, held, send_sem, recv_sem):
    place = ring_place(lax.axis_index(WIDE), size)
    left = ring_device((place + size - 1) % size, size)
    right = ring_device((place + 1) % size, size)
    tall, wide = sum_ref.shape
    rows, width = tall // 2, wide // 2
    tile = width // 4

    def cut(way, part):
        return pl.ds(part * rows, rows), pl.ds(way * width, width)

    def compute(way, hop):
        block = ring_device((place + 2 * size - 1 - hop if way == 0 else place + 1 + hop) % size, size)
        own = pl.ds(pl.multiple_of(block * tall, tall), tall)

        def step(index, carry):
            columns = pl.ds(pl.multiple_of(way * width + index * tile, tile), tile)
            target = pl.ds(pl.multiple_of(index * tile, tile), tile)
            if flipped:
                term[way, :, target] = back_dot(left_ref[own, :], right_ref[columns, :])
            else:
                term[way, :, target] = mixed_dot(left_ref[own, :], right_ref[:, columns])
            return carry

        lax.fori_loop(0, width // tile, step, 0)

    def copy(way, hop, part):
        source = first if hop == 0 else held.at[hop - 1]
        return pltpu.make_async_remote_copy(
            src_ref=source.at[cut(way, part)],
            dst_ref=held.at[(hop, *cut(way, part))],
            send_sem=send_sem.at[way, hop, part],
            recv_sem=recv_sem.at[way, hop, part],
            device_id={WIDE: right if way == 0 else left},
            device_id_type=MESH,
        )

    enter_ring(left, right)
    sent = {}
    for hop in range(size):
        for way in range(2):
            compute(way, hop)
        for part in range(2):
            for way in range(2):
                total = term[way, pl.ds(part * rows, rows), :]
                if hop:
                    sent[way, hop - 1, part].wait_recv()
                    total += held[(hop - 1, *cut(way, part))].astype(jnp.float32)
                if hop == size - 1:
                    sum_ref[cut(way, part)] = total
                    continue
                source = first if hop == 0 else held.at[hop - 1]
                source[cut(way, part)] = total.astype(jnp.bfloat16)
                sent[way, hop, part] = copy(way, hop, part)
                sent[way, hop, part].start()
    for transfer in sent.values():
        transfer.wait_send()


def scatter_rows(left, right, size, flipped, identity):
    rows = left.shape[0] // size
    width = right.shape[0 if flipped else 1]
    steps = size - 1
    return pl.pallas_call(
        functools.partial(scatter_kernel, size, flipped),
        out_shape=jax.ShapeDtypeStruct((rows, width), jnp.float32),
        in_specs=[pl.BlockSpec(memory_space=pltpu.VMEM)] * 2,
        out_specs=pl.BlockSpec(memory_space=pltpu.VMEM),
        scratch_shapes=[
            pltpu.VMEM((2, rows, width // 2), jnp.float32),
            pltpu.VMEM((rows, width), jnp.bfloat16),
            pltpu.VMEM((steps, rows, width), jnp.bfloat16),
            pltpu.SemaphoreType.DMA((2, steps, 2)),
            pltpu.SemaphoreType.DMA((2, steps, 2)),
        ],
        compiler_params=pltpu.CompilerParams(collective_id=identity, has_side_effects=True),
        cost_estimate=RING_COST,
        name="scatter_rows",
    )(left, right)


def by_column(weights, wide):
    pieces = [w.reshape(w.shape[0], wide, w.shape[1] // wide) for w in weights]
    return jnp.swapaxes(jnp.concatenate(pieces, axis=2), 0, 1)


def to_columns(block):
    block = lax.all_to_all(block, WIDE, split_axis=0, concat_axis=0, tiled=True)
    full = lax.all_gather(block, NARROW, axis=1, tiled=True)
    return full.reshape(-1, full.shape[2])


def sum_blocks(columns, wide):
    rows, width = columns.shape
    block = columns.astype(jnp.bfloat16).reshape(wide, rows // wide, width)
    return lax.psum_scatter(block, NARROW, scatter_dimension=1, tiled=True)


def to_rows(block):
    return lax.all_to_all(block, WIDE, split_axis=0, concat_axis=0, tiled=True)


def own_rows(block, start, width):
    piece = block[:, :, start : start + width]
    return jnp.swapaxes(piece, 0, 1).reshape(piece.shape[1], -1).astype(jnp.float32)


def gather_narrow(weight):
    return lax.all_gather(weight, NARROW, axis=0, tiled=True)


def sum_narrow(partial):
    return lax.psum_scatter(
        partial.astype(jnp.bfloat16), NARROW, scatter_dimension=0, tiled=True
    ).astype(jnp.float32)


def rotate_heads(values, cosine, sine_table):
    half_size = HEAD_DIM // 2
    front_half = values[..., :half_size]
    back_half = values[..., half_size:]
    return jnp.concatenate(
        [
            front_half * cosine - back_half * sine_table,
            back_half * cosine + front_half * sine_table,
        ],
        axis=-1,
    )


def split_plan(
    wide,
    narrow,
    tokens,
    lengths,
    cotangent,
    norm1_gain,
    query_weight,
    key_weight,
    value_weight,
    out_weight,
    norm2_gain,
    gate_weight,
    up_weight,
    down_weight,
):
    micro_count, length, width = tokens.shape
    rows = micro_count * length
    sequences = wide * micro_count
    heads = width // HEAD_DIM // wide
    head_width = heads * HEAD_DIM
    hidden_width = gate_weight.shape[1] // wide
    position = jnp.arange(length, dtype=jnp.int32)
    row_mask = (position[None, :] < lengths).astype(jnp.float32).reshape(rows, 1)

    share = norm1_gain.shape[0]
    gains = jnp.concatenate([norm1_gain, norm2_gain])[None]
    gains = lax.all_to_all(
        jnp.broadcast_to(gains, (wide * narrow, 2 * share)),
        AXES,
        split_axis=0,
        concat_axis=0,
        tiled=True,
    ).astype(jnp.float32)
    gains = (gains[:, :share].reshape(width), gains[:, share:].reshape(width))
    attend_columns = to_columns(by_column((query_weight, key_weight, value_weight), wide))

    floats = tokens.reshape(rows, width).astype(jnp.float32)
    inverse_one = lax.rsqrt(jnp.mean(floats * floats, axis=-1, keepdims=True) + epsilon)
    normed_one = floats * inverse_one
    upstream = cotangent.reshape(rows, width).astype(jnp.float32) * row_mask
    feed_block, tokens_all, gains = lax.optimization_barrier(
        (
            by_column((gate_weight, up_weight), wide),
            gather_rows(tokens.reshape(rows, width), wide),
            gains,
        )
    )
    floats_all = tokens_all.astype(jnp.float32)
    inverse_all = lax.rsqrt(jnp.mean(floats_all * floats_all, axis=-1, keepdims=True) + epsilon)
    first_all = (floats_all * inverse_all * gains[0]).astype(jnp.bfloat16)
    feed_block = lax.all_to_all(feed_block, WIDE, split_axis=0, concat_axis=0, tiled=True)
    feed_shares = lax.all_gather(feed_block, NARROW)
    out_rows = gather_narrow(out_weight)
    down_rows = gather_narrow(down_weight)

    cosine, sine_table = rotation_tables(length)
    cosine, sine_table = cosine[None, :, None, :], sine_table[None, :, None, :]
    joint = mixed_dot(first_all, attend_columns)
    by_head = (sequences, length, heads, HEAD_DIM)
    queries = rotate_heads(joint[:, :head_width].reshape(by_head), cosine, sine_table).astype(
        jnp.bfloat16
    )
    keys_rot = rotate_heads(
        joint[:, head_width : 2 * head_width].reshape(by_head), cosine, sine_table
    ).astype(jnp.bfloat16)
    values_all = joint[:, 2 * head_width :].reshape(by_head).astype(jnp.bfloat16)
    scores = jnp.einsum(
        "sqhd,skhd->shqk", queries, keys_rot, preferred_element_type=jnp.float32
    ) * HEAD_DIM ** (-0.5) - math.log(length)
    causal = (position[:, None] >= position[None, :]).astype(jnp.float32)
    gates_sig = jax.nn.sigmoid(scores)
    weights_low = (gates_sig * causal).astype(jnp.bfloat16)
    attended = (
        jnp.einsum("shqk,skhd->sqhd", weights_low, values_all, preferred_element_type=jnp.float32)
        .astype(jnp.bfloat16)
        .reshape(sequences * length, head_width)
    )
    middle = floats + scatter_rows(attended, out_rows, wide, False, 1)

    inverse_two = lax.rsqrt(jnp.mean(middle * middle, axis=-1, keepdims=True) + epsilon)
    normed_two = middle * inverse_two
    second_all = gather_rows((normed_two * gains[1]).astype(jnp.bfloat16), wide)

    upstream_all, front, grad_hidden, feed_columns = gather_and_feed(
        upstream.astype(jnp.bfloat16), second_all, feed_shares, down_rows, wide
    )
    gate_value = front[:, :hidden_width]
    up_value = front[:, hidden_width:]
    gate_sig = jax.nn.sigmoid(gate_value)
    hidden = (gate_value * gate_sig * up_value).astype(jnp.bfloat16)

    grad_gate = (
        grad_hidden * up_value * gate_sig * (1.0 + gate_value * (1.0 - gate_sig))
    ).astype(jnp.bfloat16)
    grad_up = (grad_hidden * gate_value * gate_sig).astype(jnp.bfloat16)
    grad_front = jnp.concatenate([grad_gate, grad_up], axis=1)
    down_term = outer_dot(hidden, upstream_all).astype(jnp.bfloat16)
    front_term = outer_dot(second_all, grad_front).astype(jnp.bfloat16)
    down_grad = sum_narrow(down_term)
    front_block = sum_blocks(front_term, wide)
    grad_second = scatter_rows(grad_front, feed_columns, wide, True, 3)
    front_block = to_rows(front_block)
    gate_grad = own_rows(front_block, 0, hidden_width)
    up_grad = own_rows(front_block, hidden_width, hidden_width)

    gain_two = jnp.sum(grad_second * normed_two, axis=0)
    grad_middle = upstream + norm_back(grad_second * gains[1], normed_two, inverse_two)
    middle_all = gather_rows(grad_middle.astype(jnp.bfloat16), wide)

    out_term, grad_attended = lax.optimization_barrier(
        (
            outer_dot(attended, middle_all).astype(jnp.bfloat16),
            back_dot(middle_all, out_rows).astype(jnp.bfloat16),
        )
    )
    grad_attended = grad_attended.reshape(by_head)
    out_grad = sum_narrow(out_term)
    grad_weights = jnp.einsum(
        "sqhd,skhd->shqk", grad_attended, values_all, preferred_element_type=jnp.float32
    )
    grad_values = jnp.einsum(
        "shqk,sqhd->skhd", weights_low, grad_attended, preferred_element_type=jnp.float32
    ).astype(jnp.bfloat16)
    grad_scores = (grad_weights * gates_sig * (1.0 - gates_sig) * causal).astype(jnp.bfloat16)
    scale_factor = HEAD_DIM ** (-0.5)
    query_rot = (
        jnp.einsum("shqk,skhd->sqhd", grad_scores, keys_rot, preferred_element_type=jnp.float32)
        * scale_factor
    )
    key_rot = (
        jnp.einsum("shqk,sqhd->skhd", grad_scores, queries, preferred_element_type=jnp.float32)
        * scale_factor
    )
    flat = (sequences * length, head_width)
    grad_joint = jnp.concatenate(
        [
            rotate_heads(query_rot, cosine, -sine_table).astype(jnp.bfloat16).reshape(flat),
            rotate_heads(key_rot, cosine, -sine_table).astype(jnp.bfloat16).reshape(flat),
            grad_values.reshape(flat),
        ],
        axis=1,
    )
    attend_term = outer_dot(first_all, grad_joint).astype(jnp.bfloat16)
    attend_block = sum_blocks(attend_term, wide)
    grad_first = scatter_rows(grad_joint, attend_columns, wide, True, 5)
    feed_out = scatter_rows(hidden, down_rows, wide, False, 4)
    layer_output = ((middle + feed_out) * row_mask).astype(jnp.bfloat16)
    attend_block = to_rows(attend_block)
    gain_one = jnp.sum(grad_first * normed_one, axis=0)
    input_grad = grad_middle + norm_back(grad_first * gains[0], normed_one, inverse_one)
    gain_terms = jnp.concatenate([gain_one.reshape(-1, share), gain_two.reshape(-1, share)], axis=1)
    gain_terms = lax.all_to_all(
        gain_terms, AXES, split_axis=0, concat_axis=0, tiled=True
    )
    gain_sums = jnp.sum(gain_terms, axis=0)
    return (
        layer_output.reshape(tokens.shape),
        input_grad.reshape(tokens.shape),
        gain_sums[:share],
        own_rows(attend_block, 0, head_width),
        own_rows(attend_block, head_width, head_width),
        own_rows(attend_block, 2 * head_width, head_width),
        out_grad,
        gain_sums[share:],
        gate_grad,
        up_grad,
        down_grad,
    )


def local(wide, narrow, *arrays):
    if arrays[0].shape[2] // HEAD_DIM % wide == 0:
        return split_plan(wide, narrow, *arrays)
    return gathered_plan(*arrays)


def solution(mesh):
    in_specs = (
        P(None, AXES, None),
        P(None, AXES),
        P(None, AXES, None),
        P(AXES),
        P(AXES, None),
        P(AXES, None),
        P(AXES, None),
        P(AXES, None),
        P(AXES),
        P(AXES, None),
        P(AXES, None),
        P(AXES, None),
    )
    out_specs = (
        P(None, AXES, None),
        P(None, AXES, None),
        P(AXES),
        P(AXES, None),
        P(AXES, None),
        P(AXES, None),
        P(AXES, None),
        P(AXES),
        P(AXES, None),
        P(AXES, None),
        P(AXES, None),
    )
    body = functools.partial(local, mesh.shape[WIDE], mesh.shape[NARROW])
    return jax.shard_map(body, mesh=mesh, in_specs=in_specs, out_specs=out_specs, check_vma=False)
```
